256 devices in a mesh: head: 4 (over x), ctx: 16 (over z, core), dp: 4 (over y).
Axes of the slice: x: 4, y: 4, z: 8, core: 2. Of those that a mesh axis runs over, the one named last changes fastest.
Arguments:
- inputs: bfloat16 [4, 8192, 64, 64], P('dp', 'ctx', 'head'), may hold values from -6 to 6
- step_sizes: float32 [4, 8192, 64], P('dp', 'ctx', 'head'), may hold values from 0.5 to 2
- decay_rate: float32 [64], P('head'), may hold values from 0.00012207031 to 0.05
- skip_gain: float32 [64], P('head'), may hold values from 0.5 to 1.5
- b_values: bfloat16 [4, 8192, 8, 128], P('dp', 'ctx', 'head'), may hold values from -6 to 6
- c_values: bfloat16 [4, 8192, 8, 128], P('dp', 'ctx', 'head'), may hold values from -0.0625 to 0.0625
- doc_lengths: int32 [4, 4], P('dp'), may hold values from 1 to 4096, 8192 in all within a row
- out_grad: bfloat16 [4, 8192, 64, 64], P('dp', 'ctx', 'head'), may hold values from -6 to 6
Outputs:
- grad_inputs: bfloat16 [4, 8192, 64, 64], P('dp', 'ctx', 'head')
- grad_steps: float32 [4, 8192, 64], P('dp', 'ctx', 'head')
- grad_decay: float32 [64], P('head')
- grad_skip: float32 [64], P('head')
- grad_b: bfloat16 [4, 8192, 8, 128], P('dp', 'ctx', 'head')
- grad_c: bfloat16 [4, 8192, 8, 128], P('dp', 'ctx', 'head')
The draws below stay inside these ranges and needn't reach their ends.
Inputs may be any that keep to these rules, and one draw needn't show every extreme that they name: `doc_lengths`: each row holds the lengths of the 4 documents of one packed sequence in order; they sum to 8192.
All inputs are finite; a program needn't handle non-finite values.
Results may differ from the reference program's by a relative error of at most 0.001.
Values may be sent and summed in bfloat16 or wider, within the bound.
A program may use at most 128 MiB of HBM per device.

```python
import math
import jax
import jax.numpy as jnp
import numpy as np
from jax import lax

HEADS = 64
P_SIZE = 64
N = 128
G = 8
SPAN = 256
DOCS = 4
LENGTH = 8192
SEQS = 4


def levels(stream_key, shape, shards, low, largest):
    gain = 1.0
    for dim, parts in shards:
        draws = jax.random.uniform(jax.random.fold_in(jax.random.fold_in(stream_key, 6), dim), (parts,), jnp.float32, low / len(shards), largest / len(shards))
        gain = gain * jnp.repeat(jnp.exp(draws), shape[dim] // parts).reshape((-1,) + (1,) * (len(shape) - 1 - dim))
    return gain


def length_profile(number_of, total, reach, slope):
    portions = [(1 << 20) // math.isqrt(rank ** slope) + 1 for rank in range(2, number_of + 1)]
    spare, holding = total - reach - (number_of - 1), [1] * (number_of - 1)
    while spare > 0:
        movable = [i for i in range(number_of - 1) if holding[i] < reach]
        whole, budget = sum([portions[i] for i in movable]), spare
        for i in movable:
            addition = min(reach - holding[i], max(1, budget * portions[i] // whole), spare)
            holding[i] = holding[i] + addition
            spare = spare - addition
    return np.array([reach] + holding)


def ragged_sizes(stream_key, amount, total, reach, lean):
    if amount == 2:
        one = jax.random.randint(stream_key, (), max(1, total - reach), min(reach, total - 1) + 1)
        return jnp.stack([one, total - one])
    sizes = jnp.asarray(length_profile(amount, total, reach, lean), jnp.int32)
    couples = (amount - 1) // 2
    source_of, sink = sizes[1:1 + 2 * couples:2], sizes[2:2 + 2 * couples:2]
    room = jnp.minimum(source_of - 1, reach - sink)
    passed = jax.random.randint(jax.random.fold_in(stream_key, 1), (couples,), 0, 1 << 20) % (room + 1)
    sizes = sizes.at[1:1 + 2 * couples:2].set(source_of - passed).at[2:2 + 2 * couples:2].set(sink + passed)
    return sizes[jax.random.permutation(jax.random.fold_in(stream_key, 2), amount)]


def noise(rng, dims, deviation, limit, cuts=(), kind=jnp.bfloat16):
    entries = deviation * jax.random.normal(rng, dims, jnp.float32)
    if cuts:
        entries = entries * levels(rng, dims, cuts, -0.22, 0.18)
    return jnp.clip(entries, -limit, limit).astype(kind)


def setup_inputs(seed: int = 0) -> dict:
    seeds = jax.random.split(jax.random.key(seed), 9)
    inputs = noise(seeds[0], (SEQS, LENGTH, HEADS, P_SIZE), 1.0, 6.0, ((0, 4), (1, 16), (2, 4)))
    step_sizes = jnp.clip(jnp.exp(math.log(2.0) - 1.3862944 * jax.random.uniform(seeds[1], (SEQS, LENGTH, HEADS), jnp.float32) ** levels(seeds[1], (SEQS, LENGTH, HEADS), ((0, 4), (1, 16), (2, 4)), -0.2, 0.2)), 0.5, 2.0)
    decay_rate = jnp.clip(jnp.exp(math.log(0.05) - 6.015181 * jax.random.uniform(seeds[2], (HEADS,), jnp.float32) ** levels(seeds[2], (HEADS,), ((0, 4),), -0.2, 0.2)), 0.00012207031, 0.05)
    skip_gain = jnp.clip(1.0 + 0.1 * jax.random.normal(seeds[3], (HEADS,), jnp.float32), 0.5, 1.5)
    b_values = noise(seeds[4], (SEQS, LENGTH, G, N), 1.0, 6.0, ((0, 4), (1, 16), (2, 4)))
    c_values = noise(seeds[5], (SEQS, LENGTH, G, N), (N * 64) ** -0.5, 0.0625, ((0, 4), (1, 16), (2, 4)))
    doc_lengths = jax.vmap(lambda own: ragged_sizes(own, DOCS, LENGTH, LENGTH // 2, 1))(jax.random.split(seeds[6], SEQS)).reshape((SEQS, DOCS)).astype(jnp.int32)
    out_grad = noise(seeds[7], (SEQS, LENGTH, HEADS, P_SIZE), 1.0, 6.0, ((0, 4), (1, 16), (2, 4)))
    return {"inputs": inputs, "step_sizes": step_sizes, "decay_rate": decay_rate, "skip_gain": skip_gain, "b_values": b_values, "c_values": c_values, "doc_lengths": doc_lengths, "out_grad": out_grad}


highest = lax.Precision.HIGHEST

def doc_index(lengths, first, count):
    ends = jnp.cumsum(lengths).astype(jnp.int32)
    places = (first + jnp.arange(count, dtype=jnp.int32)).astype(jnp.int32)
    return lax.optimization_barrier(jnp.sum((places[:, None] >= ends[None, :]).astype(jnp.int32), axis=1)).astype(jnp.int32)

def span_step(carry, pieces):
    state, decay_rate, skip_gain = carry
    inputs, step_sizes, b_values, c_values, segment, previous = pieces
    heads = inputs.shape[1]
    groups = b_values.shape[1]
    block_len = inputs.shape[0]
    b_heads = jnp.tile(b_values, (1, heads // groups, 1))
    c_heads = jnp.tile(c_values, (1, heads // groups, 1))
    running = jnp.cumsum(-decay_rate[None, :] * step_sizes, axis=0)
    order = jnp.arange(block_len, dtype=jnp.int32)
    allowed = (segment[:, None] == segment[None, :]) & (order[:, None] >= order[None, :])
    flipped = jnp.transpose(running)
    spread = flipped[:, :, None] - flipped[:, None, :]
    within = jnp.exp(jnp.where(allowed[None], spread, -jnp.inf))
    scores = jnp.einsum('ihn,jhn->hij', c_heads, b_heads, precision=highest)
    weights = scores * within * jnp.transpose(step_sizes)[:, None, :]
    output = jnp.einsum('hij,jhp->ihp', weights, inputs, precision=highest)
    entering = jnp.exp(running) * (segment == previous).astype(jnp.float32)[:, None]
    carried = jnp.einsum('ihn,hpn->ihp', c_heads, state, precision=highest)
    output = output + carried * entering[:, :, None] + skip_gain[None, :, None] * inputs
    tail = (segment == segment[-1]).astype(jnp.float32)
    leaving = jnp.exp(running[-1][None, :] - running) * tail[:, None] * step_sizes
    fresh = jnp.einsum('jhp,jhn->hpn', inputs * leaving[:, :, None], b_heads, precision=highest)
    state = entering[-1][:, None, None] * state + fresh
    return ((state, decay_rate, skip_gain), output)

def local_scan(inputs, step_sizes, decay_rate, skip_gain, b_values, c_values, segment, previous, state):
    count = inputs.shape[0]
    blocks = count // SPAN

    def split(array):
        return array.reshape((blocks, SPAN) + array.shape[1:])
    before = jnp.concatenate([jnp.reshape(previous, (1,)).astype(jnp.int32), segment[:-1]])
    firsts = split(before)[:, 0]
    pieces = (split(inputs), split(step_sizes), split(b_values), split(c_values), split(segment), firsts)
    final, output = lax.scan(jax.checkpoint(span_step), (state, decay_rate, skip_gain), pieces)
    return (output.reshape(inputs.shape), final[0])

def forward_pass(inputs, step_sizes, decay_rate, skip_gain, b_values, c_values, doc_lengths):
    heads = inputs.shape[2]
    width = inputs.shape[3]
    state_size = b_values.shape[3]

    def one_sequence(pieces):
        seq_inputs, seq_steps, seq_b, seq_c, lengths = pieces
        count = seq_inputs.shape[0]
        segment = doc_index(lengths, jnp.int32(0), count)
        previous = doc_index(lengths, jnp.int32(-1), 1)[0]
        start = jnp.zeros((heads, width, state_size), jnp.float32)
        output, final = local_scan(seq_inputs, seq_steps, decay_rate, skip_gain, seq_b, seq_c, segment, previous, start)
        return output
    return lax.map(one_sequence, (inputs, step_sizes, b_values, c_values, doc_lengths))

def reference(inputs, step_sizes, decay_rate, skip_gain, b_values, c_values, doc_lengths, out_grad):

    def wrapped(in_values, steps, rates, gains, b_part, c_part):
        return forward_pass(in_values, steps, rates, gains, b_part, c_part, doc_lengths)
    output, pull = jax.vjp(wrapped, inputs.astype(jnp.float32), step_sizes, decay_rate, skip_gain, b_values.astype(jnp.float32), c_values.astype(jnp.float32))
    grad_in, grad_st, grad_rate, grad_gain, grad_bv, grad_cv = pull(out_grad.astype(jnp.float32))
    return (grad_in.astype(jnp.bfloat16), grad_st, grad_rate, grad_gain, grad_bv.astype(jnp.bfloat16), grad_cv.astype(jnp.bfloat16))
```

```python
import functools

import jax
import jax.numpy as jnp
from jax import lax
from jax.experimental import pallas as pl
from jax.experimental.pallas import tpu as pltpu
from jax.sharding import PartitionSpec as P

F32 = jnp.float32
BF16 = jnp.bfloat16
MESH = pl.DeviceIdType.MESH
NN = ((1,), (0,))
NT = ((1,), (1,))
BLOCK = 256


def dot(a, b, dims):
    return lax.dot_general(a, b, (dims, ((), ())), preferred_element_type=F32)


def split(v):
    hi = v.astype(BF16)
    return hi, (v - hi.astype(F32)).astype(BF16)


def split3(v):
    hi = v.astype(BF16)
    rest = v - hi.astype(F32)
    mid = rest.astype(BF16)
    return hi, mid, (rest - mid.astype(F32)).astype(BF16)


def mm2(ah, al, b, dims):
    (ca,), (cb,) = dims
    return dot(jnp.concatenate([ah, al], ca), jnp.concatenate([b, b], cb), dims)


def mm2r(a, bh, bl, dims):
    (ca,), (cb,) = dims
    return dot(jnp.concatenate([a, a], ca), jnp.concatenate([bh, bl], cb), dims)


def mm3(ah, al, bh, bl, dims):
    (ca,), (cb,) = dims
    return dot(jnp.concatenate([ah, ah, al], ca), jnp.concatenate([bh, bl, bh], cb), dims)


def kernel(
    heads_n, ctx_n, dp_n,
    lens, meta, xt, yt, b, c,
    dx, gs, red, db, dc,
    mrecv, xall, yall, xh, xl, yh, yl, sh, sl, dh, dl, ut, vt,
    rate, delta, skip, fdel, einc, thr, emid, eend, zc, zr,
    btail, centr, own_s, own_g, fin, fout, gin, gout, dxs,
    gsend, grecv, ybuf, cbuf,
    lsem, a_send, a_recv, f_send, f_recv, g_send, g_recv, o_send, o_recv, q_send, q_recv,
    r_send, r_recv,
):
    me = lax.axis_index("head")
    at = lax.axis_index("ctx")
    dp = lax.axis_index("dp")
    T = xt.shape[2]

    barrier = pltpu.get_barrier_semaphore()
    for d in range(1, heads_n):
        pl.semaphore_signal(barrier, 1, device_id={"head": lax.rem(me + d, heads_n)}, device_id_type=MESH)
    for d in range(1, dp_n):
        pl.semaphore_signal(barrier, 1, device_id={"dp": lax.rem(dp + d, dp_n)}, device_id_type=MESH)
    for d in range(1, ctx_n):
        pl.semaphore_signal(barrier, 1, device_id={"ctx": lax.rem(at + d, ctx_n)}, device_id_type=MESH)
    pl.semaphore_wait(barrier, heads_n - 1 + dp_n - 1 + ctx_n - 1)

    def pieces(d):
        to = lax.rem(me + d, heads_n)
        out = [(meta.at[to], mrecv.at[me])]
        for source, target in ((xt, xall), (yt, yall)):
            for k in range(2):
                out.append((source.at[pl.ds(8 * k + 2 * to, 2)], target.at[me, k]))
        return to, out

    def remote(d, n):
        to, out = pieces(d)
        return pltpu.make_async_remote_copy(
            src_ref=out[n][0], dst_ref=out[n][1], send_sem=a_send.at[d, n], recv_sem=a_recv.at[d, n],
            device_id={"head": to}, device_id_type=MESH,
        )

    def arrived(d, n):
        src = lax.rem(me - d + heads_n, heads_n)
        target = ([mrecv.at[src]] + [r.at[src, k] for r in (xall, yall) for k in range(2)])[n]
        return pltpu.make_async_remote_copy(
            src_ref=target, dst_ref=target, send_sem=a_send.at[d, n], recv_sem=a_recv.at[d, n],
            device_id={"head": src}, device_id_type=MESH,
        )

    away = [d for d in (1, 3, 2) if d < heads_n]
    own_copies = [pltpu.make_async_copy(s, t, lsem.at[n]) for n, (s, t) in enumerate(pieces(0)[1])]
    for n in range(5):
        for d in away:
            remote(d, n).start()
    for copy in own_copies:
        copy.start()

    first = at * T
    ends = []
    total = jnp.int32(0)
    for n in range(lens.shape[0]):
        total = total + lens[n]
        ends.append(total)

    def document(place):
        return sum((place >= e).astype(jnp.int32) for e in ends)

    before = document(first - 1)
    last = document(first + T - 1)
    seg_n = document(first + lax.broadcasted_iota(jnp.int32, (T, 128), 0))
    for g in range(2):
        cb, bb = c[g], b[g]
        centr[g] = jnp.where(seg_n == before, cb, jnp.zeros_like(cb))
        btail[g] = jnp.where(seg_n == last, bb, jnp.zeros_like(bb))

    def allowed(s0, s1, t0, t1):
        shape = (s1 - s0, t1 - t0)
        s = s0 + lax.broadcasted_iota(jnp.int32, shape, 0)
        t = t0 + lax.broadcasted_iota(jnp.int32, shape, 1)
        return (document(first + s) == document(first + t)) & (t >= s)

    blocks = [(n * BLOCK, (n + 1) * BLOCK) for n in range(T // BLOCK)]
    for t0, t1 in blocks:
        ok = allowed(0, t1, t0, t1)
        for g in range(2):
            hi, lo = split(jnp.where(ok, dot(b[g, 0:t1, :], c[g, t0:t1, :], NT), 0.0))
            sh[g, 0:t1, t0:t1] = hi
            sl[g, 0:t1, t0:t1] = lo

    for copy in own_copies[:1]:
        copy.wait()
    for d in away:
        arrived(d, 0).wait_recv()
    facts = mrecv[...].reshape(heads_n * 8, T + 128)
    delta_v = facts[:, 0:T]
    rate_v = facts[:, T : T + 1]
    rate[...] = jnp.broadcast_to(rate_v, rate.shape)
    skip[...] = jnp.broadcast_to(facts[:, T + 1 : T + 2], skip.shape)
    delta[...] = delta_v
    i0 = lax.broadcasted_iota(jnp.int32, (T, T), 0)
    i1 = lax.broadcasted_iota(jnp.int32, (T, T), 1)
    upper = jnp.where(i0 <= i1, 1.0, 0.0).astype(BF16)
    run = dot(
        jnp.concatenate(split3(-rate_v * delta_v), 1), jnp.concatenate([upper, upper, upper], 0), NN
    )
    mid = run[:, T // 2 - 1 : T // 2]
    end = run[:, T - 1 : T]
    einc[...] = jnp.exp(run - mid)
    fdel[...] = jnp.exp(mid - run) * delta_v
    through = jnp.where(last == before, 1.0, 0.0)
    thr[...] = jnp.broadcast_to(jnp.exp(end) * through, thr.shape)
    emid[...] = jnp.broadcast_to(jnp.exp(mid), emid.shape)
    eend[...] = jnp.broadcast_to(jnp.exp(end - mid), eend.shape)

    def row(ref, src, n):
        return ref[pl.ds(pl.multiple_of(src * 8, 8), 8), :][n : n + 1, :]

    zc[...] = jnp.zeros_like(zc)
    zr[...] = jnp.zeros_like(zr)

    for which, (held, scale, hi_ref, lo_ref, mat, factor, own) in enumerate(
        ((xall, fdel, xh, xl, btail, eend, own_s), (yall, einc, yh, yl, centr, emid, own_g))
    ):
        for d in [0] + away:
            src = lax.rem(me - d + heads_n, heads_n)
            for k in range(2):
                n = 1 + 2 * which + k
                if d == 0:
                    own_copies[n].wait()
                else:
                    arrived(d, n).wait_recv()
            for g in range(2):
                for k in range(2):
                    v = held[src, k, g].astype(F32) * row(scale, src, 2 * k + g)
                    hi, lo = split(v)
                    hi_ref[g, src, k] = hi
                    lo_ref[g, src, k] = lo
                own_v = mm2(
                    hi_ref[g, src].reshape(128, T), lo_ref[g, src].reshape(128, T), mat[g], NN
                )
                for k in range(2):
                    own[g, src, pl.ds(64 * k, 64), :] = own_v[64 * k : 64 * k + 64] * row(factor, src, 2 * k + g)

    def intra(g):
        size = heads_n * 128
        xhv, xlv = xh[g].reshape(size, T), xl[g].reshape(size, T)
        yhv, ylv = yh[g].reshape(size, T), yl[g].reshape(size, T)
        xth, xtl = xhv.T, xlv.T
        for t0, t1 in blocks:
            d_v = mm3(xth[0:t1], xtl[0:t1], yhv[:, t0:t1], ylv[:, t0:t1], NN)
            hi, lo = split(jnp.where(allowed(0, t1, t0, t1), d_v, 0.0))
            dh[g, 0:t1, t0:t1] = hi
            dl[g, 0:t1, t0:t1] = lo
            vt[g, :, t0:t1] = mm3(xhv[:, 0:t1], xlv[:, 0:t1], sh[g, 0:t1, t0:t1], sl[g, 0:t1, t0:t1], NN)
            ut[g, :, t0:t1] = mm3(yhv[:, t0:], ylv[:, t0:], sh[g, t0:t1, t0:], sl[g, t0:t1, t0:], NT)

    def chain(coming, going, own, send, recv, step, is_first, is_last):
        @pl.when(is_first)
        def _():
            coming[...] = jnp.zeros_like(coming)

        for g in range(2):
            for d in [0] + away:
                src = lax.rem(me - d + heads_n, heads_n)
                n = g * heads_n + d
                copy = pltpu.make_async_remote_copy(
                    src_ref=going.at[g, src], dst_ref=coming.at[g, src],
                    send_sem=send.at[n], recv_sem=recv.at[n],
                    device_id={"ctx": lax.rem(at + step + ctx_n, ctx_n)}, device_id_type=MESH,
                )

                @pl.when(jnp.logical_not(is_first))
                def _():
                    copy.wait_recv()

                for k in range(2):
                    rows = pl.ds(64 * k, 64)
                    going[g, src, rows, :] = (
                        coming[g, src, rows, :] * row(thr, src, 2 * k + g) + own[g, src, rows, :]
                    )

                @pl.when(jnp.logical_not(is_last))
                def _():
                    copy.start()

    def chain_sent(going, coming, send, recv, step, is_last):
        @pl.when(jnp.logical_not(is_last))
        def _():
            for g in range(2):
                for d in [0] + away:
                    src = lax.rem(me - d + heads_n, heads_n)
                    n = g * heads_n + d
                    pltpu.make_async_remote_copy(
                        src_ref=going.at[g, src], dst_ref=coming.at[g, src],
                        send_sem=send.at[n], recv_sem=recv.at[n],
                        device_id={"ctx": lax.rem(at + step + ctx_n, ctx_n)}, device_id_type=MESH,
                    ).wait_send()

    def forward():
        chain(fin, fout, own_s, f_send, f_recv, 1, at == 0, at == ctx_n - 1)

    def backward():
        chain(gin, gout, own_g, g_send, g_recv, ctx_n - 1, at == ctx_n - 1, at == 0)

    early = at < ctx_n // 2

    @pl.when(early)
    def _():
        forward()

    @pl.when(jnp.logical_not(early))
    def _():
        backward()

    for g in range(2):
        intra(g)

    @pl.when(early)
    def _():
        backward()

    @pl.when(jnp.logical_not(early))
    def _():
        forward()

    def home(d, g, k):
        to = lax.rem(me - d + heads_n, heads_n)
        return pltpu.make_async_remote_copy(
            src_ref=dxs.at[to, k, g], dst_ref=dx.at[8 * k + 2 * me + g],
            send_sem=o_send.at[d, 2 * g + k], recv_sem=o_recv.at[d, 2 * g + k],
            device_id={"head": to}, device_id_type=MESH,
        )

    kept = []
    skips = {}
    for g in range(2):
        for d in away + [0]:
            src = lax.rem(me - d + heads_n, heads_n)
            grad = jnp.concatenate(
                [gin[g, src, 64 * k : 64 * k + 64, :] * row(eend, src, 2 * k + g) for k in range(2)], 0
            )
            gh, gl = split(grad)
            extra = mm2(gh, gl, btail[g], NT)
            for k in range(2):
                rows = pl.ds(pl.multiple_of(src * 128 + 64 * k, 64), 64)
                u = ut[g, rows, :] + extra[64 * k : 64 * k + 64]
                fd = row(fdel, src, 2 * k + g)
                dy = yall[src, k, g].astype(F32)
                x = xall[src, k, g].astype(F32)
                scaled = u * fd
                zc[pl.ds(src * 8 + 2 * k + g, 1), :] = jnp.sum(scaled * x, 0, keepdims=True)
                skips[d, k, g] = jnp.sum(dy * x, 0, keepdims=True)
                dxs[src, k, g] = (scaled + row(skip, src, 2 * k + g)[:, 0:1] * dy).astype(BF16)
                if d == 0:
                    copy = pltpu.make_async_copy(
                        dxs.at[src, k, g], dx.at[8 * k + 2 * me + g], lsem.at[5 + 2 * g + k]
                    )
                    copy.start()
                    kept.append(copy)
                else:
                    home(d, g, k).start()

    bounds = {}
    for g in range(2):
        states, grads = [None] * heads_n, [None] * heads_n
        for src in range(heads_n):
            parts, gparts = [], []
            for k in range(2):
                n = 2 * k + g
                rows = slice(64 * k, 64 * k + 64)
                st = fin[g, src, rows, :]
                gr = gin[g, src, rows, :]
                parts.append(st * row(emid, src, n))
                gparts.append(gr * row(eend, src, n))
                inner = jnp.sum(fout[g, src, rows, :] * gr, 0, keepdims=True)
                bounds[src, n] = jnp.sum(inner, 1, keepdims=True)
            states[src] = jnp.concatenate(parts, 0)
            grads[src] = jnp.concatenate(gparts, 0)
        state = jnp.concatenate(states, 0)
        grad = jnp.concatenate(grads, 0)
        size = heads_n * 128
        th, tl = split(state)
        v_v = vt[g] + mm2(th, tl, centr[g], NT)
        yhv, ylv = yh[g].reshape(size, T), yl[g].reshape(size, T)
        xhv, xlv = xh[g].reshape(size, T), xl[g].reshape(size, T)
        prod = v_v * (yhv.astype(F32) + ylv.astype(F32))
        for src in range(heads_n):
            for k in range(2):
                m = src * 128 + 64 * k
                zr[src * 8 + 2 * k + g : src * 8 + 2 * k + g + 1, :] = jnp.sum(
                    prod[m : m + 64], 0, keepdims=True
                )
        seg_row = document(first + lax.broadcasted_iota(jnp.int32, (1, T), 1))
        sth, stl = split(state.T)
        gth, gtl = split(grad.T)
        bt, ct = b[g].T, c[g].T
        dct = jnp.where(seg_row == before, mm3(sth, stl, yhv, ylv, NN), 0.0)
        dbt = jnp.where(seg_row == last, mm3(gth, gtl, xhv, xlv, NN), 0.0)
        for t0, t1 in blocks:
            dc_v = dct[:, t0:t1] + mm2r(bt[:, 0:t1], dh[g, 0:t1, t0:t1], dl[g, 0:t1, t0:t1], NN)
            dc[g, t0:t1, :] = dc_v.T.astype(BF16)
            db_v = dbt[:, t0:t1] + mm2r(ct[:, t0:], dh[g, t0:t1, t0:], dl[g, t0:t1, t0:], NT)
            db[g, t0:t1, :] = db_v.T.astype(BF16)

    live = lax.rem(lax.broadcasted_iota(jnp.int32, (heads_n * 8, 1), 0), 8) < 4
    zc_v = jnp.where(live, zc[...], 0.0)
    zr_v = jnp.where(live, zr[...], 0.0)
    lower = jnp.where(i0 >= i1, 1.0, 0.0).astype(BF16)
    later = dot(
        jnp.concatenate(split3(zr_v - zc_v), 1), jnp.concatenate([lower, lower, lower], 0), NN
    )
    nothing = jnp.zeros((1, 1), F32)
    bound = jnp.concatenate(
        [bounds[s, n] if n < 4 else nothing for s in range(heads_n) for n in range(8)], 0
    )
    later = later + bound
    delta_w = jnp.where(live, delta[...], 1.0)
    rate_w = jnp.where(live, rate[...][:, 0:1], 0.0)
    steps = zc_v / delta_w - rate_w * later
    decay_part = -jnp.sum(jnp.where(live, delta_w * later, 0.0), 1, keepdims=True)
    for s in range(heads_n):
        gsend[s, :, 0:T] = steps[8 * s : 8 * s + 8]
    for d in [0] + away:
        src = lax.rem(me - d + heads_n, heads_n)
        for k in range(2):
            for g in range(2):
                zr[pl.ds(src * 8 + 2 * k + g, 1), :] = skips[d, k, g]
    skip_part = jnp.sum(jnp.where(live, zr[...], 0.0), 1, keepdims=True)
    lane = lax.broadcasted_iota(jnp.int32, (heads_n * 8, 128), 1)
    both = jnp.where(lane == 0, decay_part, jnp.where(lane == 1, skip_part, 0.0))
    square = jnp.concatenate([both, jnp.zeros((128 - heads_n * 8, 128), F32)], 0)
    mine = square.T[0:8, :]

    ybuf[dp] = mine
    if dp_n > 1:
        out = []
        for d in range(1, dp_n):
            out.append(
                pltpu.make_async_remote_copy(
                    src_ref=ybuf.at[dp], dst_ref=ybuf.at[dp], send_sem=q_send.at[d], recv_sem=q_recv.at[d],
                    device_id={"dp": lax.rem(dp + d, dp_n)}, device_id_type=MESH,
                )
            )
            out[-1].start()
        for copy in out:
            copy.wait()
    summed = ybuf[0]
    for n in range(1, dp_n):
        summed = summed + ybuf[n]
    cbuf[at] = summed
    out = []
    for d in range(1, ctx_n):
        out.append(
            pltpu.make_async_remote_copy(
                src_ref=cbuf.at[at], dst_ref=cbuf.at[at],
                send_sem=q_send.at[dp_n + d], recv_sem=q_recv.at[dp_n + d],
                device_id={"ctx": lax.rem(at + d, ctx_n)}, device_id_type=MESH,
            )
        )
        out[-1].start()
    for copy in out:
        copy.wait()
    summed = cbuf[0]
    for n in range(1, ctx_n):
        summed = summed + cbuf[n]
    for s in range(heads_n):
        gsend[s, :, T:] = summed

    out = []
    for d in away:
        to = lax.rem(me + d, heads_n)
        out.append(
            pltpu.make_async_remote_copy(
                src_ref=gsend.at[to], dst_ref=grecv.at[me], send_sem=r_send.at[d], recv_sem=r_recv.at[d],
                device_id={"head": to}, device_id_type=MESH,
            )
        )
        out[-1].start()
    grecv[me] = gsend[me]
    for copy in out:
        copy.wait()
    for j in range(heads_n):
        for k in range(2):
            gs[8 * k + 2 * j : 8 * k + 2 * j + 2, :] = grecv[j, 2 * k : 2 * k + 2, 0:T]
        red[j] = grecv[j, :, T:]

    for d in away:
        for n in range(5):
            remote(d, n).wait_send()
        for g in range(2):
            for k in range(2):
                home(d, g, k).wait_send()
                src = lax.rem(me + d, heads_n)
                pltpu.make_async_remote_copy(
                    src_ref=dxs.at[src, k, g], dst_ref=dx.at[8 * k + 2 * src + g],
                    send_sem=o_send.at[d, 2 * g + k], recv_sem=o_recv.at[d, 2 * g + k],
                    device_id={"head": src}, device_id_type=MESH,
                ).wait_recv()
    for copy in kept:
        copy.wait()
    chain_sent(fout, fin, f_send, f_recv, 1, at == ctx_n - 1)
    chain_sent(gout, gin, g_send, g_recv, ctx_n - 1, at == 0)


def on_device(sizes, inputs, step_sizes, decay_rate, skip_gain, b_values, c_values, doc_lengths, out_grad):
    heads_n, ctx_n, dp_n = sizes
    T = inputs.shape[1]
    xt = inputs[0].transpose(1, 2, 0)
    yt = out_grad[0].transpose(1, 2, 0)
    rows = jnp.concatenate(
        [step_sizes[0].T, decay_rate[:, None], skip_gain[:, None], jnp.zeros((16, 126), F32)], 1
    )
    meta = rows.reshape(2, heads_n, 2, T + 128).transpose(1, 0, 2, 3).reshape(heads_n, 4, T + 128)
    meta = jnp.concatenate([meta, jnp.zeros_like(meta)], 1)
    b = b_values[0].transpose(1, 0, 2)
    c = c_values[0].transpose(1, 0, 2)
    vmem = pl.BlockSpec(memory_space=pltpu.VMEM)
    anywhere = pl.BlockSpec(memory_space=pl.ANY)
    R = heads_n * 8
    sizes_f = lambda *s: pltpu.VMEM(s, F32)
    sizes_b = lambda *s: pltpu.VMEM(s, BF16)
    dma = pltpu.SemaphoreType.DMA
    H = heads_n
    dx, gs, red, db, dc = pl.pallas_call(
        functools.partial(kernel, heads_n, ctx_n, dp_n),
        out_shape=(
            jax.ShapeDtypeStruct((4 * H, 64, T), BF16),
            jax.ShapeDtypeStruct((4 * H, T), F32),
            jax.ShapeDtypeStruct((H, 8, 128), F32),
            jax.ShapeDtypeStruct((2, T, 128), BF16),
            jax.ShapeDtypeStruct((2, T, 128), BF16),
        ),
        in_specs=[
            pl.BlockSpec(memory_space=pltpu.SMEM), anywhere, anywhere, anywhere, vmem, vmem,
        ],
        out_specs=(anywhere, vmem, vmem, vmem, vmem),
        scratch_shapes=[
            sizes_f(H, 8, T + 128),
            sizes_b(H, 2, 2, 64, T), sizes_b(H, 2, 2, 64, T),
            sizes_b(2, H, 2, 64, T), sizes_b(2, H, 2, 64, T), sizes_b(2, H, 2, 64, T), sizes_b(2, H, 2, 64, T),
            sizes_b(2, T, T), sizes_b(2, T, T), sizes_b(2, T, T), sizes_b(2, T, T),
            sizes_f(2, H * 128, T), sizes_f(2, H * 128, T),
            sizes_f(R, 128), sizes_f(R, T), sizes_f(R, 128), sizes_f(R, T), sizes_f(R, T),
            sizes_f(R, 128), sizes_f(R, 128), sizes_f(R, 128), sizes_f(R, T), sizes_f(R, T),
            sizes_b(2, T, 128), sizes_b(2, T, 128),
            sizes_f(2, H, 128, 128), sizes_f(2, H, 128, 128),
            sizes_f(2, H, 128, 128), sizes_f(2, H, 128, 128), sizes_f(2, H, 128, 128), sizes_f(2, H, 128, 128),
            sizes_b(H, 2, 2, 64, T),
            sizes_f(H, 8, T + 128), sizes_f(H, 8, T + 128),
            sizes_f(dp_n, 8, 128), sizes_f(ctx_n, 8, 128),
            dma((9,)), dma((H, 5)), dma((H, 5)),
            dma((2 * H,)), dma((2 * H,)), dma((2 * H,)), dma((2 * H,)),
            dma((H, 4)), dma((H, 4)), dma((dp_n + ctx_n,)), dma((dp_n + ctx_n,)),
            dma((H,)), dma((H,)),
        ],
        compiler_params=pltpu.CompilerParams(collective_id=0, has_side_effects=True),
        name="ssd_backward",
    )(doc_lengths[0], meta, xt, yt, b, c)
    me = lax.axis_index("head")
    sums = lax.dynamic_slice(red, (0, 0, me * 8), (heads_n, 2, 4))
    sums = sums.reshape(heads_n, 2, 2, 2).transpose(1, 2, 0, 3).reshape(2, 4 * heads_n)
    return (
        dx.transpose(2, 0, 1)[None],
        gs.T[None],
        sums[0],
        sums[1],
        db.transpose(1, 0, 2)[None],
        dc.transpose(1, 0, 2)[None],
    )


def solution(mesh):
    sizes = (mesh.shape["head"], mesh.shape["ctx"], mesh.shape["dp"])
    whole = P("dp", "ctx", "head", None)
    steps = P("dp", "ctx", "head")
    return jax.shard_map(
        functools.partial(on_device, sizes),
        mesh=mesh,
        in_specs=(whole, steps, P("head"), P("head"), whole, whole, P("dp", None), whole),
        out_specs=(whole, steps, P("head"), P("head"), whole, whole),
        check_vma=False,
    )
```

```python
import functools

import jax
import jax.numpy as jnp
from jax import lax
from jax.experimental import pallas as pl
from jax.experimental.pallas import tpu as pltpu
from jax.sharding import PartitionSpec as P

F32 = jnp.float32
BF16 = jnp.bfloat16
MESH = pl.DeviceIdType.MESH
NN = ((1,), (0,))
NT = ((1,), (1,))
BLOCK = 256


def dot(a, b, dims):
    return lax.dot_general(a, b, (dims, ((), ())), preferred_element_type=F32)


def split(v):
    hi = v.astype(BF16)
    return hi, (v - hi.astype(F32)).astype(BF16)


def split3(v):
    hi = v.astype(BF16)
    rest = v - hi.astype(F32)
    mid = rest.astype(BF16)
    return hi, mid, (rest - mid.astype(F32)).astype(BF16)


def mm2(ah, al, b, dims):
    (ca,), (cb,) = dims
    return dot(jnp.concatenate([ah, al], ca), jnp.concatenate([b, b], cb), dims)


def mm2r(a, bh, bl, dims):
    (ca,), (cb,) = dims
    return dot(jnp.concatenate([a, a], ca), jnp.concatenate([bh, bl], cb), dims)


def mm3(ah, al, bh, bl, dims):
    (ca,), (cb,) = dims
    return dot(jnp.concatenate([ah, ah, al], ca), jnp.concatenate([bh, bl, bh], cb), dims)


def kernel(
    heads_n, ctx_n, dp_n,
    lens, steps, rate_in, skip_in, xt, yt, b_in, c_in,
    dx, gs, red, db, dc,
    b, c, mbuf, mrecv, xall, yall, xh, xl, yh, yl, sh, sl, dh, dl, ut, vt,
    rate, delta, skip, fdel, einc, thr, pthr, emid, eend, zc, zr, zs,
    btail, centr, own, pown, inc, cin, cout, dxs,
    gsend, grecv, ybuf, cbuf,
    lsem, a_send, a_recv, t_send, t_recv, p_send, p_recv, c_send, c_recv, w_send, w_recv,
    o_send, o_recv, q_send, q_recv, r_send, r_recv,
):
    me = lax.axis_index("head")
    at = lax.axis_index("ctx")
    dp = lax.axis_index("dp")
    T = xt.shape[2]
    R = heads_n * 8
    core = lax.rem(at, 2)
    chip = at // 2
    chips = ctx_n // 2
    partner = at + 1 - 2 * core
    down = chips - 1 - chip
    pos = core * chip + (1 - core) * down
    other_pos = chips - 1 - pos
    is_first = pos == 0
    is_last = pos == chips - 1
    onward = lax.rem(at + 4 * core - 2 + ctx_n, ctx_n)

    barrier = pltpu.get_barrier_semaphore()
    for d in range(1, heads_n):
        pl.semaphore_signal(barrier, 1, device_id={"head": lax.rem(me + d, heads_n)}, device_id_type=MESH)
    for d in range(1, ctx_n):
        pl.semaphore_signal(barrier, 1, device_id={"ctx": lax.rem(at + d, ctx_n)}, device_id_type=MESH)
    for d in range(1, dp_n):
        pl.semaphore_signal(barrier, 1, device_id={"dp": lax.rem(dp + d, dp_n)}, device_id_type=MESH)

    def column(ref):
        n = ref.shape[1]
        eye = lax.broadcasted_iota(jnp.int32, (n, n), 0) == lax.broadcasted_iota(jnp.int32, (n, n), 1)
        return jnp.sum(jnp.where(eye, jnp.broadcast_to(ref[...], (n, n)), 0.0), 1, keepdims=True)

    lane = lax.broadcasted_iota(jnp.int32, (4 * heads_n, 128), 1)
    two = jnp.where(lane == 0, column(rate_in), jnp.where(lane == 1, column(skip_in), 0.0))
    steps_v = steps[...]
    mbuf[...] = jnp.zeros_like(mbuf)
    for j in range(heads_n):
        for k in range(2):
            n = 2 * heads_n * k + 2 * j
            mbuf[j, 2 * k : 2 * k + 2, 0:T] = steps_v[n : n + 2]
            mbuf[j, 2 * k : 2 * k + 2, T:] = two[n : n + 2]

    def pieces(d):
        to = lax.rem(me + d, heads_n)
        out = [(mbuf.at[to], mrecv.at[me])]
        for source, target in ((xt, xall), (yt, yall)):
            for k in range(2):
                out.append((source.at[pl.ds(2 * heads_n * k + 2 * to, 2)], target.at[me, k]))
        return to, out

    def remote(d, n):
        to, out = pieces(d)
        return pltpu.make_async_remote_copy(
            src_ref=out[n][0], dst_ref=out[n][1], send_sem=a_send.at[d, n], recv_sem=a_recv.at[d, n],
            device_id={"head": to}, device_id_type=MESH,
        )

    def source_of(d):
        return lax.rem(me - d + heads_n, heads_n)

    def arrived(d, n):
        src = source_of(d)
        target = ([mrecv.at[src]] + [r.at[src, k] for r in (xall, yall) for k in range(2)])[n]
        return pltpu.make_async_remote_copy(
            src_ref=target, dst_ref=target, send_sem=a_send.at[d, n], recv_sem=a_recv.at[d, n],
            device_id={"head": src}, device_id_type=MESH,
        )

    away = [d for d in (1, 3, 2) if d < heads_n]
    near, far = [0] + away[:2], away[2:]
    own_copies = {n: pltpu.make_async_copy(*pieces(0)[1][n], lsem.at[n]) for n in range(1, 5)}
    for n in (3, 4, 1, 2):
        own_copies[n].start()
    pl.semaphore_wait(barrier, heads_n - 1 + dp_n - 1 + ctx_n - 1)
    for d in away:
        remote(d, 0).start()
    for ds, ns in ((away[:2], (3, 4, 1, 2)), (far, (1, 2, 3, 4))):
        for n in ns:
            for d in ds:
                remote(d, n).start()
    mrecv[me] = mbuf[me]

    first = at * T
    ends = []
    total = jnp.int32(0)
    for n in range(lens.shape[0]):
        total = total + lens[n]
        ends.append(total)

    def document(place):
        return sum((place >= e).astype(jnp.int32) for e in ends)

    before = document(first - 1)
    last = document(first + T - 1)
    seg_n = document(first + lax.broadcasted_iota(jnp.int32, (T, 128), 0))
    for ref, pairs, kept_ref, seg in ((b, b_in, btail, last), (c, c_in, centr, before)):
        both = pairs[...].astype(F32)
        for g in range(2):
            v = both[:, g, :].astype(BF16)
            ref[g] = v
            kept_ref[g] = jnp.where(seg_n == seg, v, jnp.zeros_like(v))

    def allowed(s0, s1, t0, t1):
        shape = (s1 - s0, t1 - t0)
        s = s0 + lax.broadcasted_iota(jnp.int32, shape, 0)
        t = t0 + lax.broadcasted_iota(jnp.int32, shape, 1)
        return (document(first + s) == document(first + t)) & (t >= s)

    blocks = [(n * BLOCK, (n + 1) * BLOCK) for n in range(T // BLOCK)]
    for t0, t1 in blocks:
        ok = allowed(0, t1, t0, t1)
        for g in range(2):
            hi, lo = split(jnp.where(ok, dot(b[g, 0:t1, :], c[g, t0:t1, :], NT), 0.0))
            sh[g, 0:t1, t0:t1] = hi
            sl[g, 0:t1, t0:t1] = lo

    for d in away:
        arrived(d, 0).wait_recv()
    facts = mrecv[...].reshape(R, T + 128)
    delta_v = facts[:, 0:T]
    rate_v = facts[:, T : T + 1]
    rate[...] = jnp.broadcast_to(rate_v, rate.shape)
    skip[...] = jnp.broadcast_to(facts[:, T + 1 : T + 2], skip.shape)
    delta[...] = delta_v
    i0 = lax.broadcasted_iota(jnp.int32, (T, T), 0)
    i1 = lax.broadcasted_iota(jnp.int32, (T, T), 1)
    upper = jnp.where(i0 <= i1, 1.0, 0.0).astype(BF16)
    run = dot(
        jnp.concatenate(split3(-rate_v * delta_v), 1), jnp.concatenate([upper, upper, upper], 0), NN
    )
    mid = run[:, T // 2 - 1 : T // 2]
    end = run[:, T - 1 : T]
    einc[...] = jnp.exp(run - mid)
    fdel[...] = jnp.exp(mid - run) * delta_v
    through = jnp.where(last == before, 1.0, 0.0)
    thr[...] = jnp.broadcast_to(jnp.exp(end) * through, thr.shape)
    emid[...] = jnp.broadcast_to(jnp.exp(mid), emid.shape)
    eend[...] = jnp.broadcast_to(jnp.exp(end - mid), eend.shape)
    zc[...] = jnp.zeros_like(zc)
    zr[...] = jnp.zeros_like(zr)
    zs[...] = jnp.zeros_like(zs)
    thr_copy = pltpu.make_async_remote_copy(
        src_ref=thr, dst_ref=pthr, send_sem=t_send, recv_sem=t_recv,
        device_id={"ctx": partner}, device_id_type=MESH,
    )
    thr_copy.start()

    @pl.when(is_first)
    def _():
        cin[...] = jnp.zeros_like(cin)

    @pl.when(is_last)
    def _():
        inc[1 - core] = jnp.zeros_like(cin)

    def row(ref, src, n):
        return ref[pl.ds(pl.multiple_of(src * 8, 8), 8), :][n : n + 1, :]

    def to_partner(g, d):
        src = source_of(d)
        return pltpu.make_async_remote_copy(
            src_ref=own.at[1 - core, g, src], dst_ref=pown.at[g, src],
            send_sem=p_send.at[g, d], recv_sem=p_recv.at[g, d],
            device_id={"ctx": partner}, device_id_type=MESH,
        )

    def passed_on(g, d):
        src = source_of(d)
        return pltpu.make_async_remote_copy(
            src_ref=cin.at[g, src], dst_ref=inc.at[core, g, src],
            send_sem=w_send.at[g, d], recv_sem=w_recv.at[g, d],
            device_id={"ctx": partner}, device_id_type=MESH,
        )

    def relayed(g, d):
        src = source_of(d)
        return pltpu.make_async_remote_copy(
            src_ref=cout.at[g, src], dst_ref=cin.at[g, src],
            send_sem=c_send.at[g, d], recv_sem=c_recv.at[g, d],
            device_id={"ctx": onward}, device_id_type=MESH,
        )

    def prepare(kind, ds):
        held, scale, hi_ref, lo_ref, mat, factor = (
            (yall, einc, yh, yl, centr, emid), (xall, fdel, xh, xl, btail, eend)
        )[kind]

        def event():
            for d in ds:
                src = source_of(d)
                for k in range(2):
                    n = 3 - 2 * kind + k
                    if d == 0:
                        own_copies[n].wait()
                    else:
                        arrived(d, n).wait_recv()
                for g in range(2):
                    for k in range(2):
                        hi, lo = split(held[src, k, g].astype(F32) * row(scale, src, 2 * k + g))
                        hi_ref[g, src, k] = hi
                        lo_ref[g, src, k] = lo
                    own_v = mm2(
                        hi_ref[g, src].reshape(128, T), lo_ref[g, src].reshape(128, T), mat[g], NN
                    )
                    for k in range(2):
                        own[kind, g, src, pl.ds(64 * k, 64), :] = (
                            own_v[64 * k : 64 * k + 64] * row(factor, src, 2 * k + g)
                        )

            @pl.when(core != kind)
            def _():
                for d in ds:
                    for g in range(2):
                        to_partner(g, d).start()

        return event

    def relay(ds):
        def event():
            for d in ds:
                src = source_of(d)
                for g in range(2):
                    to_partner(g, d).wait_recv()

                    @pl.when(jnp.logical_not(is_first))
                    def _():
                        relayed(g, d).wait_recv()
                        passed_on(g, d).start()

                    for k in range(2):
                        rows = pl.ds(64 * k, 64)
                        n = 2 * k + g
                        here = cin[g, src, rows, :] * row(pthr, src, n) + pown[g, src, rows, :]
                        inc[core, g, src, rows, :] = here
                        cout[g, src, rows, :] = here * row(thr, src, n) + own[core, g, src, rows, :]

                    @pl.when(jnp.logical_not(is_last))
                    def _():
                        relayed(g, d).start()

        return event

    def heard(ds):
        @pl.when(jnp.logical_not(is_last))
        def _():
            for d in ds:
                for g in range(2):
                    passed_on(g, d).wait_recv()

    def inner_u(ds):
        def event():
            for d in ds:
                src = source_of(d)
                for g in range(2):
                    yhv, ylv = yh[g, src].reshape(128, T), yl[g, src].reshape(128, T)
                    for t0, t1 in blocks:
                        ut[g, src, :, t0:t1] = mm3(
                            yhv[:, t0:], ylv[:, t0:], sh[g, t0:t1, t0:], sl[g, t0:t1, t0:], NT
                        )

        return event

    size = heads_n * 128

    def inner_d(g):
        def event():
            xth, xtl = xh[g].reshape(size, T).T, xl[g].reshape(size, T).T
            for t0, t1 in blocks:
                d_v = mm3(
                    xth[0:t1], xtl[0:t1],
                    yh[g].reshape(size, T)[:, t0:t1], yl[g].reshape(size, T)[:, t0:t1], NN,
                )
                hi, lo = split(jnp.where(allowed(0, t1, t0, t1), d_v, 0.0))
                dh[g, 0:t1, t0:t1] = hi
                dl[g, 0:t1, t0:t1] = lo

        return event

    def inner_v(g):
        def event():
            xhv, xlv = xh[g].reshape(size, T), xl[g].reshape(size, T)
            for t0, t1 in blocks:
                vt[g, :, t0:t1] = mm3(
                    xhv[:, 0:t1], xlv[:, 0:t1], sh[g, 0:t1, t0:t1], sl[g, 0:t1, t0:t1], NN
                )

        return event

    def home(d, g, k):
        to = source_of(d)
        return pltpu.make_async_remote_copy(
            src_ref=dxs.at[to, k, g], dst_ref=dx.at[2 * heads_n * k + 2 * me + g],
            send_sem=o_send.at[d, 2 * g + k], recv_sem=o_recv.at[d, 2 * g + k],
            device_id={"head": to}, device_id_type=MESH,
        )

    def kept(g, k):
        return pltpu.make_async_copy(
            dxs.at[me, k, g], dx.at[2 * heads_n * k + 2 * me + g], lsem.at[5 + 2 * g + k]
        )

    def finish_dx(ds):
        def event():
            @pl.when(core == 1)
            def _():
                heard(ds)

            for d in ds[1:] + ds[:1]:
                src = source_of(d)
                for g in range(2):
                    grad = jnp.concatenate(
                        [
                            inc[0, g, src, 64 * k : 64 * k + 64, :] * row(eend, src, 2 * k + g)
                            for k in range(2)
                        ],
                        0,
                    )
                    gh, gl = split(grad)
                    extra = mm2(gh, gl, btail[g], NT)
                    for k in range(2):
                        n = 2 * k + g
                        u = ut[g, src, 64 * k : 64 * k + 64, :] + extra[64 * k : 64 * k + 64]
                        dy = yall[src, k, g].astype(F32)
                        x = xall[src, k, g].astype(F32)
                        scaled = u * row(fdel, src, n)
                        zc[pl.ds(src * 8 + n, 1), :] = jnp.sum(scaled * x, 0, keepdims=True)
                        zs[pl.ds(src * 8 + n, 1), :] = jnp.sum(dy * x, 0, keepdims=True)
                        dxs[src, k, g] = (scaled + row(skip, src, n)[:, 0:1] * dy).astype(BF16)
                        if d == 0:
                            kept(g, k).start()
                        else:
                            home(d, g, k).start()

        return event

    hop = 22
    timed = [
        (75, prepare(0, near)),
        (130, prepare(1, near)),
        (190, prepare(1, far)),
        (250, prepare(0, far)),
        ((1 - core) * 85 + core * 140 + hop * pos, relay(near)),
        ((1 - core) * 262 + core * 202 + hop * pos, relay(far)),
        (100 + 30 * (pos < 2).astype(jnp.int32), inner_u(near)),
        (256, inner_u(far)),
        (275, inner_d(0)),
        (285, inner_v(0)),
        (295, inner_d(1)),
        (305, inner_v(1)),
        (170 + hop * down + 15 * core, finish_dx(near)),
        (290 + hop * down + 15 * core, finish_dx(far)),
    ]
    times = [16 * jnp.int32(t) + n for n, (t, _) in enumerate(timed)]
    ranks = [sum((u < t).astype(jnp.int32) for u in times if u is not t) for t in times]
    thr_copy.wait_recv()

    def slot(n, carry):
        for rank, (_, event) in zip(ranks, timed):
            pl.when(rank == n)(event)
        return carry

    lax.fori_loop(0, len(timed), slot, 0)

    @pl.when(core == 0)
    def _():
        heard(near + far)

    bounds = {}
    for g in range(2):
        states = []
        for src in range(heads_n):
            for k in range(2):
                n = 2 * k + g
                rows = slice(64 * k, 64 * k + 64)
                st = inc[1, g, src, rows, :]
                states.append(st * row(emid, src, n))
                out_state = st * row(thr, src, n) + own[1, g, src, rows, :]
                inner = jnp.sum(out_state * inc[0, g, src, rows, :], 0, keepdims=True)
                bounds[src, n] = jnp.sum(inner, 1, keepdims=True)
        th, tl = split(jnp.concatenate(states, 0))
        v_v = vt[g] + mm2(th, tl, centr[g], NT)
        prod = v_v * (yh[g].reshape(size, T).astype(F32) + yl[g].reshape(size, T).astype(F32))
        for src in range(heads_n):
            for k in range(2):
                m = src * 128 + 64 * k
                n = src * 8 + 2 * k + g
                zr[n : n + 1, :] = jnp.sum(prod[m : m + 64], 0, keepdims=True)

    live = lax.rem(lax.broadcasted_iota(jnp.int32, (R, 1), 0), 8) < 4
    zc_v = zc[...]
    i0 = lax.broadcasted_iota(jnp.int32, (T, T), 0)
    i1 = lax.broadcasted_iota(jnp.int32, (T, T), 1)
    lower = jnp.where(i0 >= i1, 1.0, 0.0).astype(BF16)
    later = dot(
        jnp.concatenate(split3(zr[...] - zc_v), 1), jnp.concatenate([lower, lower, lower], 0), NN
    )
    nothing = jnp.zeros((1, 1), F32)
    bound = jnp.concatenate(
        [bounds[s, n] if n < 4 else nothing for s in range(heads_n) for n in range(8)], 0
    )
    later = later + bound
    delta_w = jnp.where(live, delta[...], 1.0)
    steps_g = zc_v / delta_w - rate[...][:, 0:1] * later
    decay_part = -jnp.sum(jnp.where(live, delta_w * later, 0.0), 1, keepdims=True)
    for s in range(heads_n):
        gsend[s, :, 0:T] = steps_g[8 * s : 8 * s + 8]
    skip_part = jnp.sum(zs[...], 1, keepdims=True)
    lane = lax.broadcasted_iota(jnp.int32, (R, 128), 1)
    both = jnp.where(lane == 0, decay_part, jnp.where(lane == 1, skip_part, 0.0))
    square = jnp.concatenate([both, jnp.zeros((128 - R, 128), F32)], 0)
    ybuf[dp] = square.T[0:8, :]

    def dp_copy(d):
        return pltpu.make_async_remote_copy(
            src_ref=ybuf.at[dp], dst_ref=ybuf.at[dp], send_sem=q_send.at[d], recv_sem=q_recv.at[d],
            device_id={"dp": lax.rem(dp + d, dp_n)}, device_id_type=MESH,
        )

    def ctx_copy(d):
        return pltpu.make_async_remote_copy(
            src_ref=cbuf.at[at], dst_ref=cbuf.at[at],
            send_sem=q_send.at[dp_n + d], recv_sem=q_recv.at[dp_n + d],
            device_id={"ctx": lax.rem(at + d, ctx_n)}, device_id_type=MESH,
        )

    def shares(g):
        th, tl = split(
            jnp.concatenate(
                [
                    inc[1, g, src, 64 * k : 64 * k + 64, :] * row(emid, src, 2 * k + g)
                    for src in range(heads_n)
                    for k in range(2)
                ],
                0,
            ).T
        )
        gh, gl = split(
            jnp.concatenate(
                [
                    inc[0, g, src, 64 * k : 64 * k + 64, :] * row(eend, src, 2 * k + g)
                    for src in range(heads_n)
                    for k in range(2)
                ],
                0,
            ).T
        )
        seg_row = document(first + lax.broadcasted_iota(jnp.int32, (1, T), 1))
        bt, ct = b[g].T, c[g].T
        dct = mm3(th, tl, yh[g].reshape(size, T), yl[g].reshape(size, T), NN)
        dbt = mm3(gh, gl, xh[g].reshape(size, T), xl[g].reshape(size, T), NN)
        dct = jnp.where(seg_row == before, dct, 0.0)
        dbt = jnp.where(seg_row == last, dbt, 0.0)
        dbs, dcs = [], []
        for t0, t1 in blocks:
            dc_v = dct[:, t0:t1] + mm2r(bt[:, 0:t1], dh[g, 0:t1, t0:t1], dl[g, 0:t1, t0:t1], NN)
            dcs.append(dc_v.T)
            db_v = dbt[:, t0:t1] + mm2r(ct[:, t0:], dh[g, t0:t1, t0:], dl[g, t0:t1, t0:], NT)
            dbs.append(db_v.T)
        db[g] = jnp.concatenate(dbs, 0).astype(BF16)
        dc[g] = jnp.concatenate(dcs, 0).astype(BF16)

    for d in range(1, dp_n):
        dp_copy(d).start()
    shares(0)
    for d in range(1, dp_n):
        dp_copy(d).wait()
    summed = ybuf[0]
    for n in range(1, dp_n):
        summed = summed + ybuf[n]
    cbuf[at] = summed
    for d in range(1, ctx_n):
        ctx_copy(d).start()
    shares(1)
    for d in range(1, ctx_n):
        ctx_copy(d).wait()
    summed = cbuf[0]
    for n in range(1, ctx_n):
        summed = summed + cbuf[n]
    for s in range(heads_n):
        gsend[s, :, T:] = summed

    out = []
    for d in away:
        to = lax.rem(me + d, heads_n)
        out.append(
            pltpu.make_async_remote_copy(
                src_ref=gsend.at[to], dst_ref=grecv.at[me], send_sem=r_send.at[d], recv_sem=r_recv.at[d],
                device_id={"head": to}, device_id_type=MESH,
            )
        )
        out[-1].start()
    grecv[me] = gsend[me]
    for copy in out:
        copy.wait()
    for j in range(heads_n):
        for k in range(2):
            n = 2 * heads_n * k + 2 * j
            gs[n : n + 2, :] = grecv[j, 2 * k : 2 * k + 2, 0:T]
        red[j] = grecv[j, :, T:]

    for d in away:
        for n in range(5):
            remote(d, n).wait_send()
        for g in range(2):
            for k in range(2):
                home(d, g, k).wait_send()
                src = lax.rem(me + d, heads_n)
                pltpu.make_async_remote_copy(
                    src_ref=dxs.at[src, k, g], dst_ref=dx.at[2 * heads_n * k + 2 * src + g],
                    send_sem=o_send.at[d, 2 * g + k], recv_sem=o_recv.at[d, 2 * g + k],
                    device_id={"head": src}, device_id_type=MESH,
                ).wait_recv()
    for g in range(2):
        for k in range(2):
            kept(g, k).wait()
        for d in near + far:
            to_partner(g, d).wait_send()
    thr_copy.wait_send()

    @pl.when(jnp.logical_not(is_first))
    def _():
        for g in range(2):
            for d in near + far:
                passed_on(g, d).wait_send()

    @pl.when(jnp.logical_not(is_last))
    def _():
        for g in range(2):
            for d in near + far:
                relayed(g, d).wait_send()


def finish(heads_n, dx_in, gs_in, red, db_in, dc_in, dx, gs, sums, db, dc, buf, sem_in, sem_out):
    parts = dx_in.shape[0] // 4
    ins = [
        pltpu.make_async_copy(dx_in.at[pl.ds(n * parts, parts)], buf.at[pl.ds(n * parts, parts)], sem_in.at[n])
        for n in range(4)
    ]
    outs = [
        pltpu.make_async_copy(buf.at[pl.ds(n * parts, parts)], dx.at[pl.ds(n * parts, parts)], sem_out.at[n])
        for n in range(4)
    ]
    for copy in ins:
        copy.start()
    gs[...] = gs_in[...]
    for ref, pairs in ((db_in, db), (dc_in, dc)):
        pairs[...] = jnp.stack([ref[0], ref[1]], 1)
    me = lax.axis_index("head")
    H = heads_n
    n0 = lax.broadcasted_iota(jnp.int32, (128, 128), 0)
    n1 = lax.broadcasted_iota(jnp.int32, (128, 128), 1)
    total = jnp.zeros((8, 128), F32)
    for j in range(H):
        for n in range(4):
            place = (n // 2) * 2 * H + 2 * j + n % 2
            lane = lax.broadcasted_iota(jnp.int32, (8, 128), 1)
            picked = jnp.sum(jnp.where(lane == me * 8 + n, red[j], 0.0), 1, keepdims=True)
            total = jnp.where(lane == place, picked, total)
    sums[...] = total
    for n in range(4):
        ins[n].wait()
        outs[n].start()
    for copy in outs:
        copy.wait()


def on_device(sizes, inputs, step_sizes, decay_rate, skip_gain, b_values, c_values, doc_lengths, out_grad):
    H, ctx_n, dp_n = sizes
    T = inputs.shape[1]
    R = H * 8
    vmem = pl.BlockSpec(memory_space=pltpu.VMEM)
    anywhere = pl.BlockSpec(memory_space=pl.ANY)
    f = lambda *s: pltpu.VMEM(s, F32)
    h = lambda *s: pltpu.VMEM(s, BF16)
    dma = pltpu.SemaphoreType.DMA
    raw = (
        jax.ShapeDtypeStruct((4 * H, 64, T), BF16),
        jax.ShapeDtypeStruct((4 * H, T), F32),
        jax.ShapeDtypeStruct((H, 8, 128), F32),
        jax.ShapeDtypeStruct((2, T, 128), BF16),
        jax.ShapeDtypeStruct((2, T, 128), BF16),
    )
    results = pl.pallas_call(
        functools.partial(kernel, H, ctx_n, dp_n),
        out_shape=raw,
        in_specs=[pl.BlockSpec(memory_space=pltpu.SMEM), vmem, vmem, vmem, anywhere, anywhere, vmem, vmem],
        out_specs=(anywhere, vmem, vmem, vmem, vmem),
        scratch_shapes=[
            h(2, T, 128), h(2, T, 128), f(H, 8, T + 128), f(H, 8, T + 128),
            h(H, 2, 2, 64, T), h(H, 2, 2, 64, T),
            h(2, H, 2, 64, T), h(2, H, 2, 64, T), h(2, H, 2, 64, T), h(2, H, 2, 64, T),
            h(2, T, T), h(2, T, T), h(2, T, T), h(2, T, T),
            f(2, H, 128, T), f(2, H * 128, T),
            f(R, 128), f(R, T), f(R, 128), f(R, T), f(R, T),
            f(R, 128), f(R, 128), f(R, 128), f(R, 128), f(R, T), f(R, T), f(R, T),
            h(2, T, 128), h(2, T, 128),
            f(2, 2, H, 128, 128), f(2, H, 128, 128), f(2, 2, H, 128, 128),
            f(2, H, 128, 128), f(2, H, 128, 128),
            h(H, 2, 2, 64, T),
            f(H, 8, T + 128), f(H, 8, T + 128), f(dp_n, 8, 128), f(ctx_n, 8, 128),
            dma((9,)), dma((H, 5)), dma((H, 5)), dma, dma, dma((2, H)), dma((2, H)),
            dma((2, H)), dma((2, H)), dma((2, H)), dma((2, H)),
            dma((H, 4)), dma((H, 4)), dma((dp_n + ctx_n,)), dma((dp_n + ctx_n,)),
            dma((H,)), dma((H,)),
        ],
        compiler_params=pltpu.CompilerParams(collective_id=0, has_side_effects=True),
        name="ssd_backward",
    )(
        doc_lengths[0], step_sizes[0].T, decay_rate[None], skip_gain[None],
        inputs[0].transpose(1, 2, 0), out_grad[0].transpose(1, 2, 0), b_values[0], c_values[0],
    )
    dx, gs, sums, db, dc = pl.pallas_call(
        functools.partial(finish, H),
        out_shape=(
            raw[0],
            raw[1],
            jax.ShapeDtypeStruct((8, 128), F32),
            jax.ShapeDtypeStruct((T, 2, 128), BF16),
            jax.ShapeDtypeStruct((T, 2, 128), BF16),
        ),
        in_specs=[anywhere, vmem, vmem, vmem, vmem],
        out_specs=(anywhere, vmem, vmem, vmem, vmem),
        scratch_shapes=[h(4 * H, 64, T), dma((4,)), dma((4,))],
        name="hand_over",
    )(*results)
    return (dx.transpose(2, 0, 1)[None], gs.T[None], sums[0, : 4 * H], sums[1, : 4 * H], db[None], dc[None])


def solution(mesh):
    sizes = (mesh.shape["head"], mesh.shape["ctx"], mesh.shape["dp"])
    whole = P("dp", "ctx", "head", None)
    steps = P("dp", "ctx", "head")
    return jax.shard_map(
        functools.partial(on_device, sizes),
        mesh=mesh,
        in_specs=(whole, steps, P("head"), P("head"), whole, whole, P("dp", None), whole),
        out_specs=(whole, steps, P("head"), P("head"), whole, whole),
        check_vma=False,
    )
```

```python
import functools

import jax
import jax.numpy as jnp
from jax import lax
from jax.experimental import pallas as pl
from jax.experimental.pallas import tpu as pltpu
from jax.sharding import PartitionSpec as P

F32 = jnp.float32
BF16 = jnp.bfloat16
MESH = pl.DeviceIdType.MESH
NN = ((1,), (0,))
NT = ((1,), (1,))
BLOCK = 256


def dot(a, b, dims):
    return lax.dot_general(a, b, (dims, ((), ())), preferred_element_type=F32)


def split(v):
    hi = v.astype(BF16)
    return hi, (v - hi.astype(F32)).astype(BF16)


def split3(v):
    hi = v.astype(BF16)
    rest = v - hi.astype(F32)
    mid = rest.astype(BF16)
    return hi, mid, (rest - mid.astype(F32)).astype(BF16)


def mm2(ah, al, b, dims):
    (ca,), (cb,) = dims
    return dot(jnp.concatenate([ah, al], ca), jnp.concatenate([b, b], cb), dims)


def mm2r(a, bh, bl, dims):
    (ca,), (cb,) = dims
    return dot(jnp.concatenate([a, a], ca), jnp.concatenate([bh, bl], cb), dims)


def mm3(ah, al, bh, bl, dims):
    (ca,), (cb,) = dims
    return dot(jnp.concatenate([ah, ah, al], ca), jnp.concatenate([bh, bl, bh], cb), dims)


def kernel(
    heads_n, ctx_n, dp_n,
    lens, steps, rate_in, skip_in, xt, yt, b_in, c_in,
    dx, gs, sums, db, dc,
    b, c, b_raw, c_raw, db_raw, dc_raw, mbuf, mrecv, xall, yall, xh, xl, yh, yl, sh, sl, dh, dl, ut, vt,
    rate, delta, skip, fdel, einc, thr, pthr, tchip, tprev, emid, eend, zc, zr, zs,
    btail, centr, own, pown, inc, one, one_in, two, two_in, four, cin, dxs, dbt, dct,
    bnd, gsend, grecv, ybuf, cbuf,
    lsem, a_send, a_recv, t_send, t_recv, p_send, p_recv, c_send, c_recv, w_send, w_recv,
    o_send, o_recv, q_send, q_recv, y_send, y_recv, r_send, r_recv,
):
    me = lax.axis_index("head")
    at = lax.axis_index("ctx")
    dp = lax.axis_index("dp")
    T = xt.shape[2]
    R = heads_n * 8
    core = lax.rem(at, 2)
    chip = at // 2
    chips = ctx_n // 2
    partner = at + 1 - 2 * core
    down = chips - 1 - chip
    pos = core * chip + (1 - core) * down
    onward = lax.rem(at + 4 * core - 2 + ctx_n, ctx_n)
    two_on = lax.rem(at + 8 * core - 4 + 2 * ctx_n, ctx_n)
    has_one, has_two = pos > 0, pos > 1
    to_one, to_two = pos < chips - 1, pos < chips - 2

    barrier = pltpu.get_barrier_semaphore()
    for d in range(1, heads_n):
        pl.semaphore_signal(barrier, 1, device_id={"head": lax.rem(me + d, heads_n)}, device_id_type=MESH)
    for d in range(1, ctx_n):
        pl.semaphore_signal(barrier, 1, device_id={"ctx": lax.rem(at + d, ctx_n)}, device_id_type=MESH)
    plane = [(u, v) for u in range(heads_n) for v in range(dp_n) if (u, v) != (0, 0)]
    for u, v in plane:
        if v:
            there = {"head": lax.rem(me + u, heads_n), "dp": lax.rem(dp + v, dp_n)}
            pl.semaphore_signal(barrier, 1, device_id=there, device_id_type=MESH)

    def column(ref):
        n = ref.shape[1]
        eye = lax.broadcasted_iota(jnp.int32, (n, n), 0) == lax.broadcasted_iota(jnp.int32, (n, n), 1)
        return jnp.sum(jnp.where(eye, jnp.broadcast_to(ref[...], (n, n)), 0.0), 1, keepdims=True)

    lane = lax.broadcasted_iota(jnp.int32, (4 * heads_n, 128), 1)
    pair = jnp.where(lane == 0, column(rate_in), jnp.where(lane == 1, column(skip_in), 0.0))
    steps_v = steps[...]
    mbuf[...] = jnp.zeros_like(mbuf)
    for j in range(heads_n):
        for k in range(2):
            n = 2 * heads_n * k + 2 * j
            mbuf[j, 2 * k : 2 * k + 2, 0:T] = steps_v[n : n + 2]
            mbuf[j, 2 * k : 2 * k + 2, T:] = pair[n : n + 2]

    def pieces(d):
        to = lax.rem(me + d, heads_n)
        out = [(mbuf.at[to], mrecv.at[me])]
        for source, target in ((xt, xall), (yt, yall)):
            for k in range(2):
                out.append((source.at[pl.ds(2 * heads_n * k + 2 * to, 2)], target.at[me, k]))
        return to, out

    def remote(d, n):
        to, out = pieces(d)
        return pltpu.make_async_remote_copy(
            src_ref=out[n][0], dst_ref=out[n][1], send_sem=a_send.at[d, n], recv_sem=a_recv.at[d, n],
            device_id={"head": to}, device_id_type=MESH,
        )

    def source_of(d):
        return lax.rem(me - d + heads_n, heads_n)

    def arrived(d, n):
        src = source_of(d)
        target = ([mrecv.at[src]] + [r.at[src, k] for r in (xall, yall) for k in range(2)])[n]
        return pltpu.make_async_remote_copy(
            src_ref=target, dst_ref=target, send_sem=a_send.at[d, n], recv_sem=a_recv.at[d, n],
            device_id={"head": src}, device_id_type=MESH,
        )

    away = [d for d in (1, 3, 2) if d < heads_n]
    own_d, near, far = [0], away[:2], away[2:]
    own_copies = {n: pltpu.make_async_copy(*pieces(0)[1][n], lsem.at[n]) for n in range(1, 5)}
    for n in (3, 4, 1, 2):
        own_copies[n].start()
    raw_copies = [
        pltpu.make_async_copy(b_in, b_raw, lsem.at[9]),
        pltpu.make_async_copy(c_in, c_raw, lsem.at[10]),
    ]
    for copy in raw_copies:
        copy.start()
    pl.semaphore_wait(barrier, len(plane) + ctx_n - 1)
    for d in away:
        remote(d, 0).start()
    for ds, ns in ((near, (3, 4)), (near, (1, 2)), (far, (3, 4)), (far, (1, 2))):
        for n in ns:
            for d in ds:
                remote(d, n).start()
    mrecv[me] = mbuf[me]

    first = at * T
    ends = []
    total = jnp.int32(0)
    for n in range(lens.shape[0]):
        total = total + lens[n]
        ends.append(total)

    def document(place):
        return sum((place >= e).astype(jnp.int32) for e in ends)

    before = document(first - 1)
    last = document(first + T - 1)
    seg_n = document(first + lax.broadcasted_iota(jnp.int32, (T, 128), 0))
    for copy in raw_copies:
        copy.wait()
    for ref, pairs, kept_ref, seg in ((b, b_raw, btail, last), (c, c_raw, centr, before)):
        both = pairs[...].astype(F32)
        for g in range(2):
            v = both[:, g, :].astype(BF16)
            ref[g] = v
            kept_ref[g] = jnp.where(seg_n == seg, v, jnp.zeros_like(v))

    def allowed(s0, s1, t0, t1):
        shape = (s1 - s0, t1 - t0)
        s = s0 + lax.broadcasted_iota(jnp.int32, shape, 0)
        t = t0 + lax.broadcasted_iota(jnp.int32, shape, 1)
        return (document(first + s) == document(first + t)) & (t >= s)

    blocks = [(n * BLOCK, (n + 1) * BLOCK) for n in range(T // BLOCK)]
    for t0, t1 in blocks:
        ok = allowed(0, t1, t0, t1)
        for g in range(2):
            hi, lo = split(jnp.where(ok, dot(b[g, 0:t1, :], c[g, t0:t1, :], NT), 0.0))
            sh[g, 0:t1, t0:t1] = hi
            sl[g, 0:t1, t0:t1] = lo

    for d in away:
        arrived(d, 0).wait_recv()
    facts = mrecv[...].reshape(R, T + 128)
    delta_v = facts[:, 0:T]
    rate_v = facts[:, T : T + 1]
    rate[...] = jnp.broadcast_to(rate_v, rate.shape)
    skip[...] = jnp.broadcast_to(facts[:, T + 1 : T + 2], skip.shape)
    delta[...] = delta_v
    i0 = lax.broadcasted_iota(jnp.int32, (T, T), 0)
    i1 = lax.broadcasted_iota(jnp.int32, (T, T), 1)
    upper = jnp.where(i0 <= i1, 1.0, 0.0).astype(BF16)
    run = dot(
        jnp.concatenate(split3(-rate_v * delta_v), 1), jnp.concatenate([upper, upper, upper], 0), NN
    )
    mid = run[:, T // 2 - 1 : T // 2]
    end = run[:, T - 1 : T]
    einc[...] = jnp.exp(run - mid)
    fdel[...] = jnp.exp(mid - run) * delta_v
    through = jnp.where(last == before, 1.0, 0.0)
    thr[...] = jnp.broadcast_to(jnp.exp(end) * through, thr.shape)
    emid[...] = jnp.broadcast_to(jnp.exp(mid), emid.shape)
    eend[...] = jnp.broadcast_to(jnp.exp(end - mid), eend.shape)
    zc[...] = jnp.zeros_like(zc)
    zr[...] = jnp.zeros_like(zr)
    zs[...] = jnp.zeros_like(zs)
    bnd[...] = jnp.zeros_like(bnd)
    thr_copy = pltpu.make_async_remote_copy(
        src_ref=thr, dst_ref=pthr, send_sem=t_send.at[0], recv_sem=t_recv.at[0],
        device_id={"ctx": partner}, device_id_type=MESH,
    )
    thr_copy.start()
    through_copy = pltpu.make_async_remote_copy(
        src_ref=tchip, dst_ref=tprev, send_sem=t_send.at[1], recv_sem=t_recv.at[1],
        device_id={"ctx": onward}, device_id_type=MESH,
    )

    @pl.when(jnp.logical_not(has_one))
    def _():
        one_in[...] = jnp.zeros_like(one_in)
        cin[...] = jnp.zeros_like(cin)
        tprev[...] = jnp.zeros_like(tprev)

    @pl.when(jnp.logical_not(has_two))
    def _():
        two_in[...] = jnp.zeros_like(two_in)

    @pl.when(jnp.logical_not(to_one))
    def _():
        inc[1 - core] = jnp.zeros_like(cin)

    def row(ref, src, n):
        return ref[pl.ds(pl.multiple_of(src * 8, 8), 8), :][n : n + 1, :]

    def to_partner(g, d):
        src = source_of(d)
        return pltpu.make_async_remote_copy(
            src_ref=own.at[1 - core, g, src], dst_ref=pown.at[g, src],
            send_sem=p_send.at[g, d], recv_sem=p_recv.at[g, d],
            device_id={"ctx": partner}, device_id_type=MESH,
        )

    def passed_on(g, d, k):
        src = source_of(d)
        rows = pl.ds(64 * k, 64)
        return pltpu.make_async_remote_copy(
            src_ref=cin.at[g, src, rows], dst_ref=inc.at[core, g, src, rows],
            send_sem=w_send.at[g, d, k], recv_sem=w_recv.at[g, d, k],
            device_id={"ctx": partner}, device_id_type=MESH,
        )

    hops = ((one, one_in, onward), (two, two_in, two_on), (four, cin, onward))

    def hop_copy(h, g, d, k):
        source, target, to = hops[h]
        src = source_of(d)
        rows = pl.ds(64 * k, 64)
        return pltpu.make_async_remote_copy(
            src_ref=source.at[g, src, rows], dst_ref=target.at[g, src, rows],
            send_sem=c_send.at[h, g, d, k], recv_sem=c_recv.at[h, g, d, k],
            device_id={"ctx": to}, device_id_type=MESH,
        )

    def each(ds, body):
        for d in ds:
            for g in range(2):
                for k in range(2):
                    body(g, d, k, source_of(d), pl.ds(64 * k, 64), 2 * k + g)

    def hop_one(ds):
        def body(g, d, k, src, rows, n):
            if k == 0:
                to_partner(g, d).wait_recv()
            one[g, src, rows, :] = pown[g, src, rows, :] * row(thr, src, n) + own[core, g, src, rows, :]
            pl.when(to_one)(lambda: hop_copy(0, g, d, k).start())

        each(ds, body)

    def hop_two(ds):
        def body(g, d, k, src, rows, n):
            pl.when(has_one)(lambda: hop_copy(0, g, d, k).wait_recv())
            two[g, src, rows, :] = one_in[g, src, rows, :] * row(tchip, src, n) + one[g, src, rows, :]
            pl.when(to_two)(lambda: hop_copy(1, g, d, k).start())

        each(ds, body)

    def hop_four(ds):
        def body(g, d, k, src, rows, n):
            pl.when(has_two)(lambda: hop_copy(1, g, d, k).wait_recv())
            both = row(tchip, src, n) * row(tprev, src, n)
            four[g, src, rows, :] = two_in[g, src, rows, :] * both + two[g, src, rows, :]
            pl.when(to_one)(lambda: hop_copy(2, g, d, k).start())

        each(ds, body)

    def hop_last(ds):
        def body(g, d, k, src, rows, n):
            @pl.when(has_one)
            def _():
                hop_copy(2, g, d, k).wait_recv()
                passed_on(g, d, k).start()

            inc[core, g, src, rows, :] = cin[g, src, rows, :] * row(pthr, src, n) + pown[g, src, rows, :]

        each(ds, body)

    def prepare(kind, ds):
        held, scale, hi_ref, lo_ref, mat, factor = (
            (yall, einc, yh, yl, centr, emid), (xall, fdel, xh, xl, btail, eend)
        )[kind]

        def event():
            for d in ds:
                src = source_of(d)
                for k in range(2):
                    n = 3 - 2 * kind + k
                    if d == 0:
                        own_copies[n].wait()
                    else:
                        arrived(d, n).wait_recv()
                for g in range(2):
                    for k in range(2):
                        hi, lo = split(held[src, k, g].astype(F32) * row(scale, src, 2 * k + g))
                        hi_ref[g, src, k] = hi
                        lo_ref[g, src, k] = lo
                    own_v = mm2(
                        hi_ref[g, src].reshape(128, T), lo_ref[g, src].reshape(128, T), mat[g], NN
                    )
                    for k in range(2):
                        own[kind, g, src, pl.ds(64 * k, 64), :] = (
                            own_v[64 * k : 64 * k + 64] * row(factor, src, 2 * k + g)
                        )

            @pl.when(core != kind)
            def _():
                for d in ds:
                    for g in range(2):
                        to_partner(g, d).start()

        return event

    def heard(ds):
        @pl.when(to_one)
        def _():
            for d in ds:
                for g in range(2):
                    for k in range(2):
                        passed_on(g, d, k).wait_recv()

    def inner_u(ds):
        def event():
            for d in ds:
                src = source_of(d)
                for g in range(2):
                    yhv, ylv = yh[g, src].reshape(128, T), yl[g, src].reshape(128, T)
                    for t0, t1 in blocks:
                        ut[g, src, :, t0:t1] = mm3(
                            yhv[:, t0:], ylv[:, t0:], sh[g, t0:t1, t0:], sl[g, t0:t1, t0:], NT
                        )

        return event

    size = heads_n * 128

    def inner_d(g):
        def event():
            xth, xtl = xh[g].reshape(size, T).T, xl[g].reshape(size, T).T
            for t0, t1 in blocks:
                d_v = mm3(
                    xth[0:t1], xtl[0:t1],
                    yh[g].reshape(size, T)[:, t0:t1], yl[g].reshape(size, T)[:, t0:t1], NN,
                )
                hi, lo = split(jnp.where(allowed(0, t1, t0, t1), d_v, 0.0))
                dh[g, 0:t1, t0:t1] = hi
                dl[g, 0:t1, t0:t1] = lo

        return event

    def inner_v(ds):
        def event():
            for d in ds:
                src = source_of(d)
                for g in range(2):
                    xhv, xlv = xh[g, src].reshape(128, T), xl[g, src].reshape(128, T)
                    for t0, t1 in blocks:
                        vt[g, src, :, t0:t1] = mm3(
                            xhv[:, 0:t1], xlv[:, 0:t1], sh[g, 0:t1, t0:t1], sl[g, 0:t1, t0:t1], NN
                        )

        return event

    def finish_rows(ds):
        def event():
            @pl.when(core == 0)
            def _():
                heard(ds)

            for d in ds:
                src = source_of(d)
                for g in range(2):
                    state = jnp.concatenate(
                        [
                            inc[1, g, src, 64 * k : 64 * k + 64, :] * row(emid, src, 2 * k + g)
                            for k in range(2)
                        ],
                        0,
                    )
                    th, tl = split(state)
                    v_v = vt[g, src] + mm2(th, tl, centr[g], NT)
                    for k in range(2):
                        n = 2 * k + g
                        y_v = yh[g, src, k].astype(F32) + yl[g, src, k].astype(F32)
                        prod = v_v[64 * k : 64 * k + 64] * y_v
                        zr[pl.ds(src * 8 + n, 1), :] = jnp.sum(prod, 0, keepdims=True)
                        x = xall[src, k, g].astype(F32)
                        scaled = ut[g, src, 64 * k : 64 * k + 64, :]
                        zc[pl.ds(src * 8 + n, 1), :] = jnp.sum(scaled * x, 0, keepdims=True)
                        dy = yall[src, k, g].astype(F32)
                        zs[pl.ds(src * 8 + n, 1), :] = jnp.sum(dy * x, 0, keepdims=True)
                        rows = slice(64 * k, 64 * k + 64)
                        out_state = inc[1, g, src, rows, :] * row(thr, src, n) + own[1, g, src, rows, :]
                        bnd[pl.ds(src * 8 + n, 1), :] = jnp.sum(
                            out_state * inc[0, g, src, rows, :], 0, keepdims=True
                        )

        return event

    def inner_bc(g):
        bt, ct = b[g].T, c[g].T
        for t0, t1 in blocks:
            dct[g, :, t0:t1] = mm2r(bt[:, 0:t1], dh[g, 0:t1, t0:t1], dl[g, 0:t1, t0:t1], NN)
            dbt[g, :, t0:t1] = mm2r(ct[:, t0:], dh[g, t0:t1, t0:], dl[g, t0:t1, t0:], NT)

    def outer_bc(kind, g):
        inside, factor, hi_ref, lo_ref, seg = ((dbt, eend, xh, xl, last), (dct, emid, yh, yl, before))[kind]
        hi, lo = split(
            jnp.concatenate(
                [
                    inc[kind, g, src, 64 * k : 64 * k + 64, :] * row(factor, src, 2 * k + g)
                    for src in range(heads_n)
                    for k in range(2)
                ],
                0,
            ).T
        )
        seg_row = document(first + lax.broadcasted_iota(jnp.int32, (1, T), 1))
        outside = mm3(hi, lo, hi_ref[g].reshape(size, T), lo_ref[g].reshape(size, T), NN)
        return (inside[g] + jnp.where(seg_row == seg, outside, 0.0)).T.astype(BF16)

    def share(kind):
        raw, out = ((db_raw, db), (dc_raw, dc))[kind]
        raw[...] = jnp.stack([outer_bc(kind, 0), outer_bc(kind, 1)], 1)
        copy = pltpu.make_async_copy(raw, out, lsem.at[9 + kind])
        copy.start()
        return copy

    def home(d, g, k):
        to = source_of(d)
        return pltpu.make_async_remote_copy(
            src_ref=dxs.at[to, k, g], dst_ref=dx.at[2 * heads_n * k + 2 * me + g],
            send_sem=o_send.at[d, 2 * g + k], recv_sem=o_recv.at[d, 2 * g + k],
            device_id={"head": to}, device_id_type=MESH,
        )

    def kept(g, k):
        return pltpu.make_async_copy(
            dxs.at[me, k, g], dx.at[2 * heads_n * k + 2 * me + g], lsem.at[5 + 2 * g + k]
        )

    def finish_dx(ds):
        def event():
            @pl.when(core == 1)
            def _():
                heard(ds)

            for d in ds[1:] + ds[:1]:
                src = source_of(d)
                for g in range(2):
                    grad = jnp.concatenate(
                        [
                            inc[0, g, src, 64 * k : 64 * k + 64, :] * row(eend, src, 2 * k + g)
                            for k in range(2)
                        ],
                        0,
                    )
                    gh, gl = split(grad)
                    extra = mm2(gh, gl, btail[g], NT)
                    for k in range(2):
                        n = 2 * k + g
                        u = ut[g, src, 64 * k : 64 * k + 64, :] + extra[64 * k : 64 * k + 64]
                        dy = yall[src, k, g].astype(F32)
                        scaled = u * row(fdel, src, n)
                        ut[g, src, 64 * k : 64 * k + 64, :] = scaled
                        dxs[src, k, g] = (scaled + row(skip, src, n)[:, 0:1] * dy).astype(BF16)
                        if d == 0:
                            kept(g, k).start()
                        else:
                            home(d, g, k).start()

        return event

    down_core, up_core = core == 0, core == 1

    def on(which, event, ds):
        pl.when(which)(lambda: event(ds))

    prepare(0, own_d)()
    prepare(1, own_d)()
    thr_copy.wait_recv()
    tchip[...] = thr[...] * pthr[...]
    pl.when(to_one)(through_copy.start)
    hop_one(own_d)
    inner_u(own_d)()
    inner_v(own_d)()
    prepare(0, near)()
    hop_two(own_d)
    on(down_core, hop_one, near)
    pl.when(has_one)(through_copy.wait_recv)
    inner_u(near)()
    hop_four(own_d)
    on(down_core, hop_two, near)
    prepare(1, near)()
    hop_last(own_d)
    on(up_core, hop_one, near)
    on(down_core, hop_four, near)
    inner_v(near)()
    prepare(0, far)()
    on(down_core, hop_last, near)
    on(up_core, hop_two, near)
    on(down_core, hop_one, far)
    finish_dx(own_d)()
    inner_u(far)()
    on(up_core, hop_four, near)
    on(down_core, hop_two, far)
    prepare(1, far)()
    on(up_core, hop_one, far)
    on(up_core, hop_last, near)
    on(down_core, hop_four, far)
    finish_dx(near)()
    finish_rows(own_d)()
    inner_v(far)()
    on(down_core, hop_last, far)
    on(up_core, hop_two, far)
    inner_d(0)()
    finish_dx(far)()
    on(up_core, hop_four, far)
    inner_d(1)()
    finish_rows(near)()
    inner_bc(0)
    inner_bc(1)
    on(up_core, hop_last, far)
    finish_rows(far)()

    live = lax.rem(lax.broadcasted_iota(jnp.int32, (R, 1), 0), 8) < 4
    zc_v = zc[...]
    i0 = lax.broadcasted_iota(jnp.int32, (T, T), 0)
    i1 = lax.broadcasted_iota(jnp.int32, (T, T), 1)
    lower = jnp.where(i0 >= i1, 1.0, 0.0).astype(BF16)
    later = dot(
        jnp.concatenate(split3(zr[...] - zc_v), 1), jnp.concatenate([lower, lower, lower], 0), NN
    )
    later = later + jnp.sum(bnd[...], 1, keepdims=True)
    delta_w = jnp.where(live, delta[...], 1.0)
    steps_g = zc_v / delta_w - rate[...][:, 0:1] * later
    decay_part = -jnp.sum(jnp.where(live, delta_w * later, 0.0), 1, keepdims=True)
    for s in range(heads_n):
        gsend[s] = steps_g[8 * s : 8 * s + 8]
    skip_part = jnp.sum(zs[...], 1, keepdims=True)
    lane = lax.broadcasted_iota(jnp.int32, (R, 128), 1)
    both = jnp.where(lane == 0, decay_part, jnp.where(lane == 1, skip_part, 0.0))
    square = jnp.concatenate([both, jnp.zeros((128 - R, 128), F32)], 0)
    ybuf[dp, me] = square.T[0:8, :]

    def plane_copy(n):
        u, v = plane[n]
        return pltpu.make_async_remote_copy(
            src_ref=ybuf.at[dp, me], dst_ref=ybuf.at[dp, me], send_sem=y_send.at[n], recv_sem=y_recv.at[n],
            device_id={"head": lax.rem(me + u, heads_n), "dp": lax.rem(dp + v, dp_n)}, device_id_type=MESH,
        )

    def ctx_copy(d):
        return pltpu.make_async_remote_copy(
            src_ref=cbuf.at[at], dst_ref=cbuf.at[at], send_sem=q_send.at[d], recv_sem=q_recv.at[d],
            device_id={"ctx": lax.rem(at + d, ctx_n)}, device_id_type=MESH,
        )

    def steps_home(d):
        to = lax.rem(me + d, heads_n)
        return pltpu.make_async_remote_copy(
            src_ref=gsend.at[to], dst_ref=grecv.at[me], send_sem=r_send.at[d], recv_sem=r_recv.at[d],
            device_id={"head": to}, device_id_type=MESH,
        )

    for n in range(len(plane)):
        plane_copy(n).start()
    for d in away:
        steps_home(d).start()
    grecv[me] = gsend[me]
    out_copies = [share(0)]
    for n in range(len(plane)):
        plane_copy(n).wait()
    lane8 = lax.broadcasted_iota(jnp.int32, (8, 128), 1)
    mine = jnp.zeros((8, 128), F32)
    for j in range(heads_n):
        whole = ybuf[0, j]
        for n in range(1, dp_n):
            whole = whole + ybuf[n, j]
        for n in range(4):
            place = (n // 2) * 2 * heads_n + 2 * j + n % 2
            picked = jnp.sum(jnp.where(lane8 == me * 8 + n, whole, 0.0), 1, keepdims=True)
            mine = jnp.where(lane8 == place, picked, mine)
    cbuf[at] = mine
    for d in range(1, ctx_n):
        ctx_copy(d).start()
    out_copies.append(share(1))
    for d in away:
        steps_home(d).wait()
    for j in range(heads_n):
        for k in range(2):
            n = 2 * heads_n * k + 2 * j
            gs[n : n + 2, :] = grecv[j, 2 * k : 2 * k + 2]
    for d in range(1, ctx_n):
        ctx_copy(d).wait()
    summed = cbuf[0]
    for n in range(1, ctx_n):
        summed = summed + cbuf[n]
    sums[...] = summed

    for d in away:
        for n in range(5):
            remote(d, n).wait_send()
        for g in range(2):
            for k in range(2):
                home(d, g, k).wait_send()
                src = lax.rem(me + d, heads_n)
                pltpu.make_async_remote_copy(
                    src_ref=dxs.at[src, k, g], dst_ref=dx.at[2 * heads_n * k + 2 * src + g],
                    send_sem=o_send.at[d, 2 * g + k], recv_sem=o_recv.at[d, 2 * g + k],
                    device_id={"head": src}, device_id_type=MESH,
                ).wait_recv()
    for g in range(2):
        for k in range(2):
            kept(g, k).wait()
        for d in own_d + near + far:
            to_partner(g, d).wait_send()
    thr_copy.wait_send()
    for copy in out_copies:
        copy.wait()
    everything = own_d + near + far
    pl.when(has_one)(lambda: each(everything, lambda g, d, k, *_: passed_on(g, d, k).wait_send()))
    pl.when(to_one)(through_copy.wait_send)
    for h, sent in enumerate((to_one, to_two, to_one)):
        pl.when(sent)(lambda: each(everything, lambda g, d, k, *_: hop_copy(h, g, d, k).wait_send()))


def finish(count, dx_in, gs_in, sums, db_in, dc_in, dx, gs, decay, gain, db, dc, x_buf, b_buf, c_buf, sem_in, sem_out):
    parts = dx_in.shape[0] // 4
    moves = [(dx_in.at[pl.ds(n * parts, parts)], x_buf.at[n], dx.at[pl.ds(n * parts, parts)]) for n in range(4)]
    moves += [(db_in, b_buf, db), (dc_in, c_buf, dc)]
    ins = [pltpu.make_async_copy(a, m, sem_in.at[n]) for n, (a, m, z) in enumerate(moves)]
    outs = [pltpu.make_async_copy(m, z, sem_out.at[n]) for n, (a, m, z) in enumerate(moves)]
    for copy in ins:
        copy.start()
    gs[...] = gs_in[...]
    decay[...] = sums[0:1, 0:count]
    gain[...] = sums[1:2, 0:count]
    for a, z in zip(ins, outs):
        a.wait()
        z.start()
    for copy in outs:
        copy.wait()


def on_device(sizes, inputs, step_sizes, decay_rate, skip_gain, b_values, c_values, doc_lengths, out_grad):
    H, ctx_n, dp_n = sizes
    T = inputs.shape[1]
    R = H * 8
    vmem = pl.BlockSpec(memory_space=pltpu.VMEM)
    anywhere = pl.BlockSpec(memory_space=pl.ANY)
    f = lambda *s: pltpu.VMEM(s, F32)
    h = lambda *s: pltpu.VMEM(s, BF16)
    dma = pltpu.SemaphoreType.DMA
    raw = (
        jax.ShapeDtypeStruct((4 * H, 64, T), BF16),
        jax.ShapeDtypeStruct((4 * H, T), F32),
        jax.ShapeDtypeStruct((8, 128), F32),
        jax.ShapeDtypeStruct((T, 2, 128), BF16),
        jax.ShapeDtypeStruct((T, 2, 128), BF16),
    )
    results = pl.pallas_call(
        functools.partial(kernel, H, ctx_n, dp_n),
        out_shape=raw,
        in_specs=[pl.BlockSpec(memory_space=pltpu.SMEM), vmem, vmem, vmem] + [anywhere] * 4,
        out_specs=(anywhere, vmem, vmem, anywhere, anywhere),
        scratch_shapes=[
            h(2, T, 128), h(2, T, 128), h(T, 2, 128), h(T, 2, 128), h(T, 2, 128), h(T, 2, 128),
            f(H, 8, T + 128), f(H, 8, T + 128),
            h(H, 2, 2, 64, T), h(H, 2, 2, 64, T),
            h(2, H, 2, 64, T), h(2, H, 2, 64, T), h(2, H, 2, 64, T), h(2, H, 2, 64, T),
            h(2, T, T), h(2, T, T), h(2, T, T), h(2, T, T),
            f(2, H, 128, T), f(2, H, 128, T),
            f(R, 128), f(R, T), f(R, 128), f(R, T), f(R, T),
            f(R, 128), f(R, 128), f(R, 128), f(R, 128), f(R, 128), f(R, 128), f(R, T), f(R, T), f(R, T),
            h(2, T, 128), h(2, T, 128),
            f(2, 2, H, 128, 128), f(2, H, 128, 128), f(2, 2, H, 128, 128),
            f(2, H, 128, 128), f(2, H, 128, 128), f(2, H, 128, 128), f(2, H, 128, 128),
            f(2, H, 128, 128), f(2, H, 128, 128),
            h(H, 2, 2, 64, T), f(2, 128, T), f(2, 128, T),
            f(R, 128), f(H, 8, T), f(H, 8, T), f(dp_n, H, 8, 128), f(ctx_n, 8, 128),
            dma((11,)), dma((H, 5)), dma((H, 5)), dma((2,)), dma((2,)), dma((2, H)), dma((2, H)),
            dma((3, 2, H, 2)), dma((3, 2, H, 2)), dma((2, H, 2)), dma((2, H, 2)),
            dma((H, 4)), dma((H, 4)), dma((ctx_n,)), dma((ctx_n,)),
            dma((H * dp_n,)), dma((H * dp_n,)), dma((H,)), dma((H,)),
        ],
        compiler_params=pltpu.CompilerParams(collective_id=0, has_side_effects=True),
        name="ssd_backward",
    )(
        doc_lengths[0], step_sizes[0].T, decay_rate[None], skip_gain[None],
        inputs[0].transpose(1, 2, 0), out_grad[0].transpose(1, 2, 0), b_values[0], c_values[0],
    )
    dx, gs, decay, gain, db, dc = pl.pallas_call(
        functools.partial(finish, 4 * H),
        out_shape=raw[:2] + (jax.ShapeDtypeStruct((1, 4 * H), F32),) * 2 + raw[3:],
        in_specs=[anywhere, vmem, vmem, anywhere, anywhere],
        out_specs=(anywhere, vmem, vmem, vmem, anywhere, anywhere),
        scratch_shapes=[h(4, H, 64, T), h(T, 2, 128), h(T, 2, 128), dma((6,)), dma((6,))],
        name="hand_over",
    )(*results)
    return (dx.transpose(2, 0, 1)[None], gs.T[None], decay[0], gain[0], db[None], dc[None])


def solution(mesh):
    sizes = (mesh.shape["head"], mesh.shape["ctx"], mesh.shape["dp"])
    whole = P("dp", "ctx", "head", None)
    steps = P("dp", "ctx", "head")
    return jax.shard_map(
        functools.partial(on_device, sizes),
        mesh=mesh,
        in_specs=(whole, steps, P("head"), P("head"), whole, whole, P("dp", None), whole),
        out_specs=(whole, steps, P("head"), P("head"), whole, whole),
        check_vma=False,
    )
```

```python
import functools

import jax
import jax.numpy as jnp
from jax import lax
from jax.experimental import pallas as pl
from jax.experimental.pallas import tpu as pltpu
from jax.sharding import PartitionSpec as P

F32 = jnp.float32
BF16 = jnp.bfloat16
MESH = pl.DeviceIdType.MESH
NN = ((1,), (0,))
NT = ((1,), (1,))
BLOCK = 256


def dot(a, b, dims):
    return lax.dot_general(a, b, (dims, ((), ())), preferred_element_type=F32)


def split(v):
    hi = v.astype(BF16)
    return hi, (v - hi.astype(F32)).astype(BF16)


def split3(v):
    hi = v.astype(BF16)
    rest = v - hi.astype(F32)
    mid = rest.astype(BF16)
    return hi, mid, (rest - mid.astype(F32)).astype(BF16)


def mm2(ah, al, b, dims):
    (ca,), (cb,) = dims
    return dot(jnp.concatenate([ah, al], ca), jnp.concatenate([b, b], cb), dims)


def mm2r(a, bh, bl, dims):
    (ca,), (cb,) = dims
    return dot(jnp.concatenate([a, a], ca), jnp.concatenate([bh, bl], cb), dims)


def mm3(ah, al, bh, bl, dims):
    (ca,), (cb,) = dims
    return dot(jnp.concatenate([ah, ah, al], ca), jnp.concatenate([bh, bl, bh], cb), dims)


def kernel(
    heads_n, ctx_n, dp_n,
    lens, steps, rate_in, skip_in, xt, yt, b_in, c_in,
    dx, gs, sums, db, dc,
    b, c, b_raw, c_raw, db_raw, dc_raw, mbuf, mrecv, xall, yall, xh, xl, yh, yl, sh, sl, dh, dl, ut, vt,
    rate, delta, skip, fdel, einc, thr, pthr, tchip, tprev, emid, eend, zc, zr, zs,
    btail, centr, own, pown, inc, one, one_in, two, two_in, four, cin, dxs, dbt, dct,
    bnd, gsend, grecv, ybuf, cbuf,
    lsem, a_send, a_recv, t_send, t_recv, p_send, p_recv, c_send, c_recv, w_send, w_recv,
    o_send, o_recv, q_send, q_recv, y_send, y_recv, r_send, r_recv,
):
    me = lax.axis_index("head")
    at = lax.axis_index("ctx")
    dp = lax.axis_index("dp")
    T = xt.shape[2]
    R = heads_n * 8
    core = lax.rem(at, 2)
    chip = at // 2
    chips = ctx_n // 2
    partner = at + 1 - 2 * core
    down = chips - 1 - chip
    pos = core * chip + (1 - core) * down
    onward = lax.rem(at + 4 * core - 2 + ctx_n, ctx_n)
    two_on = lax.rem(at + 8 * core - 4 + 2 * ctx_n, ctx_n)
    has_one, has_two = pos > 0, pos > 1
    to_one, to_two = pos < chips - 1, pos < chips - 2

    barrier = pltpu.get_barrier_semaphore()
    for d in range(1, heads_n):
        pl.semaphore_signal(barrier, 1, device_id={"head": lax.rem(me + d, heads_n)}, device_id_type=MESH)
    for d in range(1, ctx_n):
        pl.semaphore_signal(barrier, 1, device_id={"ctx": lax.rem(at + d, ctx_n)}, device_id_type=MESH)
    plane = [(u, v) for u in range(heads_n) for v in range(dp_n) if (u, v) != (0, 0)]
    for u, v in plane:
        if v:
            there = {"head": lax.rem(me + u, heads_n), "dp": lax.rem(dp + v, dp_n)}
            pl.semaphore_signal(barrier, 1, device_id=there, device_id_type=MESH)

    def column(ref):
        n = ref.shape[1]
        eye = lax.broadcasted_iota(jnp.int32, (n, n), 0) == lax.broadcasted_iota(jnp.int32, (n, n), 1)
        return jnp.sum(jnp.where(eye, jnp.broadcast_to(ref[...], (n, n)), 0.0), 1, keepdims=True)

    lane = lax.broadcasted_iota(jnp.int32, (4 * heads_n, 128), 1)
    pair = jnp.where(lane == 0, column(rate_in), jnp.where(lane == 1, column(skip_in), 0.0))
    steps_v = steps[...]
    mbuf[...] = jnp.zeros_like(mbuf)
    for j in range(heads_n):
        for k in range(2):
            n = 2 * heads_n * k + 2 * j
            mbuf[j, 2 * k : 2 * k + 2, 0:T] = steps_v[n : n + 2]
            mbuf[j, 2 * k : 2 * k + 2, T:] = pair[n : n + 2]

    def pieces(d):
        to = lax.rem(me + d, heads_n)
        out = [(mbuf.at[to], mrecv.at[me])]
        for source, target in ((xt, xall), (yt, yall)):
            for k in range(2):
                out.append((source.at[pl.ds(2 * heads_n * k + 2 * to, 2)], target.at[me, k]))
        return to, out

    def remote(d, n):
        to, out = pieces(d)
        return pltpu.make_async_remote_copy(
            src_ref=out[n][0], dst_ref=out[n][1], send_sem=a_send.at[d, n], recv_sem=a_recv.at[d, n],
            device_id={"head": to}, device_id_type=MESH,
        )

    def source_of(d):
        return lax.rem(me - d + heads_n, heads_n)

    def arrived(d, n):
        src = source_of(d)
        target = ([mrecv.at[src]] + [r.at[src, k] for r in (xall, yall) for k in range(2)])[n]
        return pltpu.make_async_remote_copy(
            src_ref=target, dst_ref=target, send_sem=a_send.at[d, n], recv_sem=a_recv.at[d, n],
            device_id={"head": src}, device_id_type=MESH,
        )

    away = [d for d in (1, 3, 2) if d < heads_n]
    own_d, near, far = [0], away[:2], away[2:]
    own_copies = {n: pltpu.make_async_copy(*pieces(0)[1][n], lsem.at[n]) for n in range(1, 5)}
    for n in (3, 4, 1, 2):
        own_copies[n].start()
    raw_copies = [
        pltpu.make_async_copy(b_in, b_raw, lsem.at[9]),
        pltpu.make_async_copy(c_in, c_raw, lsem.at[10]),
    ]
    for copy in raw_copies:
        copy.start()
    pl.semaphore_wait(barrier, len(plane) + ctx_n - 1)
    for d in away:
        remote(d, 0).start()
    for ds, ns in ((near, (3, 4)), (near, (1, 2)), (far, (3, 4)), (far, (1, 2))):
        for n in ns:
            for d in ds:
                remote(d, n).start()
    mrecv[me] = mbuf[me]

    first = at * T
    ends = []
    total = jnp.int32(0)
    for n in range(lens.shape[0]):
        total = total + lens[n]
        ends.append(total)

    def document(place):
        return sum((place >= e).astype(jnp.int32) for e in ends)

    before = document(first - 1)
    last = document(first + T - 1)
    seg_n = document(first + lax.broadcasted_iota(jnp.int32, (T, 128), 0))
    for copy in raw_copies:
        copy.wait()
    for ref, pairs, kept_ref, seg in ((b, b_raw, btail, last), (c, c_raw, centr, before)):
        both = pairs[...].astype(F32)
        for g in range(2):
            v = both[:, g, :].astype(BF16)
            ref[g] = v
            kept_ref[g] = jnp.where(seg_n == seg, v, jnp.zeros_like(v))

    def allowed(s0, s1, t0, t1):
        shape = (s1 - s0, t1 - t0)
        s = s0 + lax.broadcasted_iota(jnp.int32, shape, 0)
        t = t0 + lax.broadcasted_iota(jnp.int32, shape, 1)
        return (document(first + s) == document(first + t)) & (t >= s)

    blocks = [(n * BLOCK, (n + 1) * BLOCK) for n in range(T // BLOCK)]
    for t0, t1 in blocks:
        ok = allowed(0, t1, t0, t1)
        for g in range(2):
            hi, lo = split(jnp.where(ok, dot(b[g, 0:t1, :], c[g, t0:t1, :], NT), 0.0))
            sh[g, 0:t1, t0:t1] = hi
            sl[g, 0:t1, t0:t1] = lo

    for d in away:
        arrived(d, 0).wait_recv()
    facts = mrecv[...].reshape(R, T + 128)
    delta_v = facts[:, 0:T]
    rate_v = facts[:, T : T + 1]
    rate[...] = jnp.broadcast_to(rate_v, rate.shape)
    skip[...] = jnp.broadcast_to(facts[:, T + 1 : T + 2], skip.shape)
    delta[...] = delta_v
    i0 = lax.broadcasted_iota(jnp.int32, (T, T), 0)
    i1 = lax.broadcasted_iota(jnp.int32, (T, T), 1)
    upper = jnp.where(i0 <= i1, 1.0, 0.0).astype(BF16)
    run = dot(
        jnp.concatenate(split3(-rate_v * delta_v), 1), jnp.concatenate([upper, upper, upper], 0), NN
    )
    mid = run[:, T // 2 - 1 : T // 2]
    end = run[:, T - 1 : T]
    einc[...] = jnp.exp(run - mid)
    fdel[...] = jnp.exp(mid - run) * delta_v
    through = jnp.where(last == before, 1.0, 0.0)
    thr[...] = jnp.broadcast_to(jnp.exp(end) * through, thr.shape)
    emid[...] = jnp.broadcast_to(jnp.exp(mid), emid.shape)
    eend[...] = jnp.broadcast_to(jnp.exp(end - mid), eend.shape)
    zc[...] = jnp.zeros_like(zc)
    zr[...] = jnp.zeros_like(zr)
    zs[...] = jnp.zeros_like(zs)
    bnd[...] = jnp.zeros_like(bnd)
    thr_copy = pltpu.make_async_remote_copy(
        src_ref=thr, dst_ref=pthr, send_sem=t_send.at[0], recv_sem=t_recv.at[0],
        device_id={"ctx": partner}, device_id_type=MESH,
    )
    thr_copy.start()
    through_copy = pltpu.make_async_remote_copy(
        src_ref=tchip, dst_ref=tprev, send_sem=t_send.at[1], recv_sem=t_recv.at[1],
        device_id={"ctx": onward}, device_id_type=MESH,
    )

    @pl.when(jnp.logical_not(has_one))
    def _():
        one_in[...] = jnp.zeros_like(one_in)
        cin[...] = jnp.zeros_like(cin)
        tprev[...] = jnp.zeros_like(tprev)

    @pl.when(jnp.logical_not(has_two))
    def _():
        two_in[...] = jnp.zeros_like(two_in)

    @pl.when(jnp.logical_not(to_one))
    def _():
        inc[1 - core] = jnp.zeros_like(cin)

    def row(ref, src, n):
        return ref[pl.ds(pl.multiple_of(src * 8, 8), 8), :][n : n + 1, :]

    def to_partner(g, d):
        src = source_of(d)
        return pltpu.make_async_remote_copy(
            src_ref=own.at[1 - core, g, src], dst_ref=pown.at[g, src],
            send_sem=p_send.at[g, d], recv_sem=p_recv.at[g, d],
            device_id={"ctx": partner}, device_id_type=MESH,
        )

    def passed_on(g, d, k):
        src = source_of(d)
        rows = pl.ds(64 * k, 64)
        return pltpu.make_async_remote_copy(
            src_ref=cin.at[g, src, rows], dst_ref=inc.at[core, g, src, rows],
            send_sem=w_send.at[g, d, k], recv_sem=w_recv.at[g, d, k],
            device_id={"ctx": partner}, device_id_type=MESH,
        )

    hops = ((one, one_in, onward), (two, two_in, two_on), (four, cin, onward))

    def hop_copy(h, g, d, k):
        source, target, to = hops[h]
        src = source_of(d)
        rows = pl.ds(64 * k, 64)
        return pltpu.make_async_remote_copy(
            src_ref=source.at[g, src, rows], dst_ref=target.at[g, src, rows],
            send_sem=c_send.at[h, g, d, k], recv_sem=c_recv.at[h, g, d, k],
            device_id={"ctx": to}, device_id_type=MESH,
        )

    def each(ds, body):
        for d in ds:
            for g in range(2):
                for k in range(2):
                    body(g, d, k, source_of(d), pl.ds(64 * k, 64), 2 * k + g)

    def hop_one(ds):
        def body(g, d, k, src, rows, n):
            if k == 0:
                to_partner(g, d).wait_recv()
            one[g, src, rows, :] = pown[g, src, rows, :] * row(thr, src, n) + own[core, g, src, rows, :]
            pl.when(to_one)(lambda: hop_copy(0, g, d, k).start())

        each(ds, body)

    def hop_two(ds):
        def body(g, d, k, src, rows, n):
            pl.when(has_one)(lambda: hop_copy(0, g, d, k).wait_recv())
            two[g, src, rows, :] = one_in[g, src, rows, :] * row(tchip, src, n) + one[g, src, rows, :]
            pl.when(to_two)(lambda: hop_copy(1, g, d, k).start())

        each(ds, body)

    def hop_four(ds):
        def body(g, d, k, src, rows, n):
            pl.when(has_two)(lambda: hop_copy(1, g, d, k).wait_recv())
            both = row(tchip, src, n) * row(tprev, src, n)
            four[g, src, rows, :] = two_in[g, src, rows, :] * both + two[g, src, rows, :]
            pl.when(to_one)(lambda: hop_copy(2, g, d, k).start())

        each(ds, body)

    def hop_last(ds):
        def body(g, d, k, src, rows, n):
            @pl.when(has_one)
            def _():
                hop_copy(2, g, d, k).wait_recv()
                passed_on(g, d, k).start()

            inc[core, g, src, rows, :] = cin[g, src, rows, :] * row(pthr, src, n) + pown[g, src, rows, :]

        each(ds, body)

    def prepare(kind, ds):
        held, scale, hi_ref, lo_ref, mat, factor = (
            (yall, einc, yh, yl, centr, emid), (xall, fdel, xh, xl, btail, eend)
        )[kind]

        def event():
            for d in ds:
                src = source_of(d)
                for k in range(2):
                    n = 3 - 2 * kind + k
                    if d == 0:
                        own_copies[n].wait()
                    else:
                        arrived(d, n).wait_recv()
                for g in range(2):
                    for k in range(2):
                        hi, lo = split(held[src, k, g].astype(F32) * row(scale, src, 2 * k + g))
                        hi_ref[g, src, k] = hi
                        lo_ref[g, src, k] = lo
                    own_v = mm2(
                        hi_ref[g, src].reshape(128, T), lo_ref[g, src].reshape(128, T), mat[g], NN
                    )
                    for k in range(2):
                        own[kind, g, src, pl.ds(64 * k, 64), :] = (
                            own_v[64 * k : 64 * k + 64] * row(factor, src, 2 * k + g)
                        )

            @pl.when(core != kind)
            def _():
                for d in ds:
                    for g in range(2):
                        to_partner(g, d).start()

        return event

    def heard(ds):
        @pl.when(to_one)
        def _():
            for d in ds:
                for g in range(2):
                    for k in range(2):
                        passed_on(g, d, k).wait_recv()

    def rows_of(ref, g, ds):
        return jnp.concatenate([ref[g, source_of(d)].reshape(128, T) for d in ds], 0)

    def put(ref, g, ds, t0, t1, v):
        for n, d in enumerate(ds):
            ref[g, source_of(d), :, t0:t1] = v[128 * n : 128 * n + 128]

    def inner_u(ds):
        def event():
            for g in range(2):
                yhv, ylv = rows_of(yh, g, ds), rows_of(yl, g, ds)
                for t0, t1 in blocks:
                    v = mm3(yhv[:, t0:], ylv[:, t0:], sh[g, t0:t1, t0:], sl[g, t0:t1, t0:], NT)
                    put(ut, g, ds, t0, t1, v)

        return event

    size = heads_n * 128

    def inner_d(g):
        def event():
            xth, xtl = xh[g].reshape(size, T).T, xl[g].reshape(size, T).T
            for t0, t1 in blocks:
                d_v = mm3(
                    xth[0:t1], xtl[0:t1],
                    yh[g].reshape(size, T)[:, t0:t1], yl[g].reshape(size, T)[:, t0:t1], NN,
                )
                hi, lo = split(jnp.where(allowed(0, t1, t0, t1), d_v, 0.0))
                dh[g, 0:t1, t0:t1] = hi
                dl[g, 0:t1, t0:t1] = lo

        return event

    def inner_v(ds):
        def event():
            for g in range(2):
                xhv, xlv = rows_of(xh, g, ds), rows_of(xl, g, ds)
                for t0, t1 in blocks:
                    v = mm3(xhv[:, 0:t1], xlv[:, 0:t1], sh[g, 0:t1, t0:t1], sl[g, 0:t1, t0:t1], NN)
                    put(vt, g, ds, t0, t1, v)

        return event

    def finish_rows(ds):
        def event():
            @pl.when(core == 0)
            def _():
                heard(ds)

            for d in ds:
                src = source_of(d)
                for g in range(2):
                    state = jnp.concatenate(
                        [
                            inc[1, g, src, 64 * k : 64 * k + 64, :] * row(emid, src, 2 * k + g)
                            for k in range(2)
                        ],
                        0,
                    )
                    th, tl = split(state)
                    v_v = vt[g, src] + mm2(th, tl, centr[g], NT)
                    for k in range(2):
                        n = 2 * k + g
                        y_v = yh[g, src, k].astype(F32) + yl[g, src, k].astype(F32)
                        prod = v_v[64 * k : 64 * k + 64] * y_v
                        zr[pl.ds(src * 8 + n, 1), :] = jnp.sum(prod, 0, keepdims=True)
                        x = xall[src, k, g].astype(F32)
                        scaled = ut[g, src, 64 * k : 64 * k + 64, :]
                        zc[pl.ds(src * 8 + n, 1), :] = jnp.sum(scaled * x, 0, keepdims=True)
                        dy = yall[src, k, g].astype(F32)
                        zs[pl.ds(src * 8 + n, 1), :] = jnp.sum(dy * x, 0, keepdims=True)
                        rows = slice(64 * k, 64 * k + 64)
                        out_state = inc[1, g, src, rows, :] * row(thr, src, n) + own[1, g, src, rows, :]
                        bnd[pl.ds(src * 8 + n, 1), :] = jnp.sum(
                            out_state * inc[0, g, src, rows, :], 0, keepdims=True
                        )

        return event

    def inner_bc(g):
        bt, ct = b[g].T, c[g].T
        for t0, t1 in blocks:
            dct[g, :, t0:t1] = mm2r(bt[:, 0:t1], dh[g, 0:t1, t0:t1], dl[g, 0:t1, t0:t1], NN)
            dbt[g, :, t0:t1] = mm2r(ct[:, t0:], dh[g, t0:t1, t0:], dl[g, t0:t1, t0:], NT)

    def outer_bc(kind, g):
        inside, factor, hi_ref, lo_ref, seg = ((dbt, eend, xh, xl, last), (dct, emid, yh, yl, before))[kind]
        hi, lo = split(
            jnp.concatenate(
                [
                    inc[kind, g, src, 64 * k : 64 * k + 64, :] * row(factor, src, 2 * k + g)
                    for src in range(heads_n)
                    for k in range(2)
                ],
                0,
            ).T
        )
        seg_row = document(first + lax.broadcasted_iota(jnp.int32, (1, T), 1))
        outside = mm3(hi, lo, hi_ref[g].reshape(size, T), lo_ref[g].reshape(size, T), NN)
        return (inside[g] + jnp.where(seg_row == seg, outside, 0.0)).T.astype(BF16)

    def share(kind):
        raw, out = ((db_raw, db), (dc_raw, dc))[kind]
        raw[...] = jnp.stack([outer_bc(kind, 0), outer_bc(kind, 1)], 1)
        copy = pltpu.make_async_copy(raw, out, lsem.at[9 + kind])
        copy.start()
        return copy

    def home(d, g, k):
        to = source_of(d)
        return pltpu.make_async_remote_copy(
            src_ref=dxs.at[to, k, g], dst_ref=dx.at[2 * heads_n * k + 2 * me + g],
            send_sem=o_send.at[d, 2 * g + k], recv_sem=o_recv.at[d, 2 * g + k],
            device_id={"head": to}, device_id_type=MESH,
        )

    def kept(g, k):
        return pltpu.make_async_copy(
            dxs.at[me, k, g], dx.at[2 * heads_n * k + 2 * me + g], lsem.at[5 + 2 * g + k]
        )

    def finish_dx(ds):
        def event():
            @pl.when(core == 1)
            def _():
                heard(ds)

            for d in ds[1:] + ds[:1]:
                src = source_of(d)
                for g in range(2):
                    grad = jnp.concatenate(
                        [
                            inc[0, g, src, 64 * k : 64 * k + 64, :] * row(eend, src, 2 * k + g)
                            for k in range(2)
                        ],
                        0,
                    )
                    gh, gl = split(grad)
                    extra = mm2(gh, gl, btail[g], NT)
                    for k in range(2):
                        n = 2 * k + g
                        u = ut[g, src, 64 * k : 64 * k + 64, :] + extra[64 * k : 64 * k + 64]
                        dy = yall[src, k, g].astype(F32)
                        scaled = u * row(fdel, src, n)
                        ut[g, src, 64 * k : 64 * k + 64, :] = scaled
                        dxs[src, k, g] = (scaled + row(skip, src, n)[:, 0:1] * dy).astype(BF16)
                        if d == 0:
                            kept(g, k).start()
                        else:
                            home(d, g, k).start()

        return event

    down_core, up_core = core == 0, core == 1

    def on(which, event, ds):
        pl.when(which)(lambda: event(ds))

    prepare(0, own_d)()
    prepare(1, own_d)()
    thr_copy.wait_recv()
    tchip[...] = thr[...] * pthr[...]
    pl.when(to_one)(through_copy.start)
    hop_one(own_d)
    prepare(0, near)()
    hop_two(own_d)
    on(down_core, hop_one, near)
    pl.when(has_one)(through_copy.wait_recv)
    inner_u(own_d + near)()
    hop_four(own_d)
    on(down_core, hop_two, near)
    prepare(1, near)()
    hop_last(own_d)
    on(up_core, hop_one, near)
    on(down_core, hop_four, near)
    inner_v(own_d + near)()
    prepare(0, far)()
    on(down_core, hop_last, near)
    on(up_core, hop_two, near)
    on(down_core, hop_one, far)
    finish_dx(own_d)()
    inner_u(far)()
    on(up_core, hop_four, near)
    on(down_core, hop_two, far)
    prepare(1, far)()
    on(up_core, hop_one, far)
    on(up_core, hop_last, near)
    on(down_core, hop_four, far)
    finish_dx(near)()
    finish_rows(own_d)()
    inner_v(far)()
    on(down_core, hop_last, far)
    on(up_core, hop_two, far)
    inner_d(0)()
    finish_dx(far)()
    on(up_core, hop_four, far)
    inner_d(1)()
    finish_rows(near)()
    inner_bc(0)
    inner_bc(1)
    on(up_core, hop_last, far)
    finish_rows(far)()

    live = lax.rem(lax.broadcasted_iota(jnp.int32, (R, 1), 0), 8) < 4
    zc_v = zc[...]
    i0 = lax.broadcasted_iota(jnp.int32, (T, T), 0)
    i1 = lax.broadcasted_iota(jnp.int32, (T, T), 1)
    lower = jnp.where(i0 >= i1, 1.0, 0.0).astype(BF16)
    later = dot(
        jnp.concatenate(split3(zr[...] - zc_v), 1), jnp.concatenate([lower, lower, lower], 0), NN
    )
    later = later + jnp.sum(bnd[...], 1, keepdims=True)
    delta_w = jnp.where(live, delta[...], 1.0)
    steps_g = zc_v / delta_w - rate[...][:, 0:1] * later
    decay_part = -jnp.sum(jnp.where(live, delta_w * later, 0.0), 1, keepdims=True)
    for s in range(heads_n):
        gsend[s] = steps_g[8 * s : 8 * s + 8]
    skip_part = jnp.sum(zs[...], 1, keepdims=True)
    lane = lax.broadcasted_iota(jnp.int32, (R, 128), 1)
    both = jnp.where(lane == 0, decay_part, jnp.where(lane == 1, skip_part, 0.0))
    square = jnp.concatenate([both, jnp.zeros((128 - R, 128), F32)], 0)
    ybuf[dp, me] = square.T[0:8, :]

    def plane_copy(n):
        u, v = plane[n]
        return pltpu.make_async_remote_copy(
            src_ref=ybuf.at[dp, me], dst_ref=ybuf.at[dp, me], send_sem=y_send.at[n], recv_sem=y_recv.at[n],
            device_id={"head": lax.rem(me + u, heads_n), "dp": lax.rem(dp + v, dp_n)}, device_id_type=MESH,
        )

    def ctx_copy(d):
        return pltpu.make_async_remote_copy(
            src_ref=cbuf.at[at], dst_ref=cbuf.at[at], send_sem=q_send.at[d], recv_sem=q_recv.at[d],
            device_id={"ctx": lax.rem(at + d, ctx_n)}, device_id_type=MESH,
        )

    def steps_home(d):
        to = lax.rem(me + d, heads_n)
        return pltpu.make_async_remote_copy(
            src_ref=gsend.at[to], dst_ref=grecv.at[me], send_sem=r_send.at[d], recv_sem=r_recv.at[d],
            device_id={"head": to}, device_id_type=MESH,
        )

    for n in range(len(plane)):
        plane_copy(n).start()
    for d in away:
        steps_home(d).start()
    grecv[me] = gsend[me]
    out_copies = [share(0)]
    for n in range(len(plane)):
        plane_copy(n).wait()
    lane8 = lax.broadcasted_iota(jnp.int32, (8, 128), 1)
    mine = jnp.zeros((8, 128), F32)
    for j in range(heads_n):
        whole = ybuf[0, j]
        for n in range(1, dp_n):
            whole = whole + ybuf[n, j]
        for n in range(4):
            place = (n // 2) * 2 * heads_n + 2 * j + n % 2
            picked = jnp.sum(jnp.where(lane8 == me * 8 + n, whole, 0.0), 1, keepdims=True)
            mine = jnp.where(lane8 == place, picked, mine)
    cbuf[at] = mine
    for d in range(1, ctx_n):
        ctx_copy(d).start()
    out_copies.append(share(1))
    for d in away:
        steps_home(d).wait()
    for j in range(heads_n):
        for k in range(2):
            n = 2 * heads_n * k + 2 * j
            gs[n : n + 2, :] = grecv[j, 2 * k : 2 * k + 2]
    for d in range(1, ctx_n):
        ctx_copy(d).wait()
    summed = cbuf[0]
    for n in range(1, ctx_n):
        summed = summed + cbuf[n]
    sums[...] = summed

    for d in away:
        for n in range(5):
            remote(d, n).wait_send()
        for g in range(2):
            for k in range(2):
                home(d, g, k).wait_send()
                src = lax.rem(me + d, heads_n)
                pltpu.make_async_remote_copy(
                    src_ref=dxs.at[src, k, g], dst_ref=dx.at[2 * heads_n * k + 2 * src + g],
                    send_sem=o_send.at[d, 2 * g + k], recv_sem=o_recv.at[d, 2 * g + k],
                    device_id={"head": src}, device_id_type=MESH,
                ).wait_recv()
    for g in range(2):
        for k in range(2):
            kept(g, k).wait()
        for d in own_d + near + far:
            to_partner(g, d).wait_send()
    thr_copy.wait_send()
    for copy in out_copies:
        copy.wait()
    everything = own_d + near + far
    pl.when(has_one)(lambda: each(everything, lambda g, d, k, *_: passed_on(g, d, k).wait_send()))
    pl.when(to_one)(through_copy.wait_send)
    for h, sent in enumerate((to_one, to_two, to_one)):
        pl.when(sent)(lambda: each(everything, lambda g, d, k, *_: hop_copy(h, g, d, k).wait_send()))


def finish(
    count, dx_in, gs_in, sums, db_in, dc_in, dx, gs, decay, gain, db, dc,
    x_buf, b_buf, c_buf, g_buf, sem_in, sem_out,
):
    parts = dx_in.shape[0] // 4
    moves = [(dx_in.at[pl.ds(n * parts, parts)], x_buf.at[n], dx.at[pl.ds(n * parts, parts)]) for n in range(4)]
    moves += [(db_in, b_buf, db), (dc_in, c_buf, dc), (gs_in, g_buf, gs)]
    ins = [pltpu.make_async_copy(a, m, sem_in.at[n]) for n, (a, m, z) in enumerate(moves)]
    outs = [pltpu.make_async_copy(m, z, sem_out.at[n]) for n, (a, m, z) in enumerate(moves)]
    for copy in ins:
        copy.start()
    decay[...] = sums[0:1, 0:count]
    gain[...] = sums[1:2, 0:count]
    for a, z in zip(ins, outs):
        a.wait()
        z.start()
    for copy in outs:
        copy.wait()


def on_device(sizes, inputs, step_sizes, decay_rate, skip_gain, b_values, c_values, doc_lengths, out_grad):
    H, ctx_n, dp_n = sizes
    T = inputs.shape[1]
    R = H * 8
    vmem = pl.BlockSpec(memory_space=pltpu.VMEM)
    anywhere = pl.BlockSpec(memory_space=pl.ANY)
    f = lambda *s: pltpu.VMEM(s, F32)
    h = lambda *s: pltpu.VMEM(s, BF16)
    dma = pltpu.SemaphoreType.DMA
    raw = (
        jax.ShapeDtypeStruct((4 * H, 64, T), BF16),
        jax.ShapeDtypeStruct((4 * H, T), F32),
        jax.ShapeDtypeStruct((8, 128), F32),
        jax.ShapeDtypeStruct((T, 2, 128), BF16),
        jax.ShapeDtypeStruct((T, 2, 128), BF16),
    )
    results = pl.pallas_call(
        functools.partial(kernel, H, ctx_n, dp_n),
        out_shape=raw,
        in_specs=[pl.BlockSpec(memory_space=pltpu.SMEM), vmem, vmem, vmem] + [anywhere] * 4,
        out_specs=(anywhere, vmem, vmem, anywhere, anywhere),
        scratch_shapes=[
            h(2, T, 128), h(2, T, 128), h(T, 2, 128), h(T, 2, 128), h(T, 2, 128), h(T, 2, 128),
            f(H, 8, T + 128), f(H, 8, T + 128),
            h(H, 2, 2, 64, T), h(H, 2, 2, 64, T),
            h(2, H, 2, 64, T), h(2, H, 2, 64, T), h(2, H, 2, 64, T), h(2, H, 2, 64, T),
            h(2, T, T), h(2, T, T), h(2, T, T), h(2, T, T),
            f(2, H, 128, T), f(2, H, 128, T),
            f(R, 128), f(R, T), f(R, 128), f(R, T), f(R, T),
            f(R, 128), f(R, 128), f(R, 128), f(R, 128), f(R, 128), f(R, 128), f(R, T), f(R, T), f(R, T),
            h(2, T, 128), h(2, T, 128),
            f(2, 2, H, 128, 128), f(2, H, 128, 128), f(2, 2, H, 128, 128),
            f(2, H, 128, 128), f(2, H, 128, 128), f(2, H, 128, 128), f(2, H, 128, 128),
            f(2, H, 128, 128), f(2, H, 128, 128),
            h(H, 2, 2, 64, T), f(2, 128, T), f(2, 128, T),
            f(R, 128), f(H, 8, T), f(H, 8, T), f(dp_n, H, 8, 128), f(ctx_n, 8, 128),
            dma((11,)), dma((H, 5)), dma((H, 5)), dma((2,)), dma((2,)), dma((2, H)), dma((2, H)),
            dma((3, 2, H, 2)), dma((3, 2, H, 2)), dma((2, H, 2)), dma((2, H, 2)),
            dma((H, 4)), dma((H, 4)), dma((ctx_n,)), dma((ctx_n,)),
            dma((H * dp_n,)), dma((H * dp_n,)), dma((H,)), dma((H,)),
        ],
        compiler_params=pltpu.CompilerParams(collective_id=0, has_side_effects=True),
        name="ssd_backward",
    )(
        doc_lengths[0], step_sizes[0].T, decay_rate[None], skip_gain[None],
        inputs[0].transpose(1, 2, 0), out_grad[0].transpose(1, 2, 0), b_values[0], c_values[0],
    )
    dx, gs, decay, gain, db, dc = pl.pallas_call(
        functools.partial(finish, 4 * H),
        out_shape=raw[:2] + (jax.ShapeDtypeStruct((1, 4 * H), F32),) * 2 + raw[3:],
        in_specs=[anywhere, anywhere, vmem, anywhere, anywhere],
        out_specs=(anywhere, anywhere, vmem, vmem, anywhere, anywhere),
        scratch_shapes=[
            h(4, H, 64, T), h(T, 2, 128), h(T, 2, 128), f(4 * H, T), dma((7,)), dma((7,)),
        ],
        name="hand_over",
    )(*results)
    return (dx.transpose(2, 0, 1)[None], gs.T[None], decay[0], gain[0], db[None], dc[None])


def solution(mesh):
    sizes = (mesh.shape["head"], mesh.shape["ctx"], mesh.shape["dp"])
    whole = P("dp", "ctx", "head", None)
    steps = P("dp", "ctx", "head")
    return jax.shard_map(
        functools.partial(on_device, sizes),
        mesh=mesh,
        in_specs=(whole, steps, P("head"), P("head"), whole, whole, P("dp", None), whole),
        out_specs=(whole, steps, P("head"), P("head"), whole, whole),
        check_vma=False,
    )
```
